256 devices in a mesh: event: 8 (over x, core), pack: 8 (over z), tensor: 4 (over y).
Axes of the slice: x: 4, y: 4, z: 8, core: 2. Of those that a mesh axis runs over, the one named last changes fastest.
Arguments:
- features: bfloat16 [32768, 1024], P(('event', 'pack', 'tensor')), may hold values from -24 to 24
- dest_owner: int32 [32768], P(('event', 'pack', 'tensor')), may hold values from 0 to 63, as said below
- dest_slot: int32 [32768], P(('event', 'pack', 'tensor')), may hold values from 0 to 127, as said below
- doc_ids: int32 [64, 512], P(('event', 'pack')), may hold values from 0 to 7, never falling along the last dimension, each value on 1 to 128 neighbouring positions
- enc_weight: bfloat16 [2, 1024, 1024], replicated, may hold values from -0.1875 to 0.1875
- attn_in: bfloat16 [4, 1024, 1024], P(None, None, 'tensor'), may hold values from -0.1875 to 0.1875
- attn_out: bfloat16 [1024, 1024], P('tensor'), may hold values from -0.1875 to 0.1875
- ffn_in: bfloat16 [2, 1024, 2048], P(None, None, 'tensor'), may hold values from -0.1875 to 0.1875
- ffn_out: bfloat16 [2048, 1024], P('tensor'), may hold values from -0.125 to 0.125
- out_grad: bfloat16 [64, 512, 1024], P(('event', 'pack'), 'tensor'), may hold values from -6 to 6
Outputs:
- packed_out: bfloat16 [64, 512, 1024], P(('event', 'pack'), 'tensor')
- row_grad: bfloat16 [32768, 1024], P(('event', 'pack', 'tensor'))
- enc_grad: float32 [2, 1024, 1024], P(None, ('event', 'pack'), 'tensor')
The draws below stay inside these ranges and needn't reach their ends.
Inputs may be any that keep to these rules, and one draw needn't show every extreme that they name: `dest_owner`: the sequence of each event, numbered over event and pack with event slowest. From the devices of one tensor index every sequence receives exactly 128 events; from one device at most 3 events go to one sequence, every device sends exactly 3 to some sequence, and every sequence receives exactly 3 from some device. `dest_slot`: events of one tensor index that go to one sequence have distinct slots, so they fill that sequence's positions tix * 128 to tix * 128 + 127. `doc_ids`: document numbers never fall along a sequence; a document holds 1 to 128 positions.
All inputs are finite; a program needn't handle non-finite values.
Results may differ from the reference program's by a relative error of at most 0.023.
Values may be sent and summed in bfloat16 or wider, within the bound.
A program may use at most 128 MiB of HBM per device.

```python
import math
import jax
import jax.numpy as jnp
import numpy as np
from jax import lax

D = 1024
HEADS = 16
FF = 2048
ENC_LAYERS = 2
ROWS_DEV = 128
SEQS = 64
LEN = 512
EVENTS = 32768
DOCS = 8
DOC_MOST = 128
N_TENSOR = 4


def route_plan(key):
    base = jax.random.fold_in(key, 11)

    def one_slice(slice_key):
        subkeys = jax.random.split(slice_key, 6)
        mean_load = ROWS_DEV // SEQS
        half_load = mean_load // 2
        spread = jax.random.randint(subkeys[0], (SEQS // 2,), 0, half_load + 1)
        spread = spread.at[0].set(half_load)
        pattern = jnp.concatenate([mean_load + spread, mean_load - spread]).astype(jnp.int32)
        pattern = pattern[jax.random.permutation(subkeys[1], SEQS)]
        shift_dst = jax.random.permutation(subkeys[2], SEQS)
        shift_src = jax.random.permutation(subkeys[3], SEQS)
        counts = pattern[(shift_dst[None, :] - shift_src[:, None]) % SEQS]
        bounds = jnp.cumsum(counts, axis=1)
        begins = bounds - counts
        ordinal = jnp.arange(ROWS_DEV, dtype=jnp.int32)
        owner_sorted = jnp.sum((ordinal[None, :, None] >= bounds[:, None, :]).astype(jnp.int32), axis=2)
        rank_sorted = ordinal[None, :] - jnp.take_along_axis(begins, owner_sorted, axis=1)
        arrive = jnp.cumsum(counts, axis=0) - counts
        position = jnp.take_along_axis(arrive, owner_sorted, axis=1) + rank_sorted
        slot_keys = jax.random.split(subkeys[4], SEQS)
        slot_perm = jax.vmap(lambda item: jax.random.permutation(item, ROWS_DEV))(slot_keys)
        slot_sorted = slot_perm[owner_sorted, position]
        row_keys = jax.random.split(subkeys[5], SEQS)
        row_perm = jax.vmap(lambda item: jax.random.permutation(item, ROWS_DEV))(row_keys)
        inverse = jnp.argsort(row_perm, axis=1)
        owners = jnp.take_along_axis(owner_sorted, inverse, axis=1)
        slots = jnp.take_along_axis(slot_sorted, inverse, axis=1)
        return (owners, slots)
    owners, slots = jax.vmap(one_slice)(jax.random.split(base, N_TENSOR))
    owners = owners.transpose(1, 0, 2).reshape(-1).astype(jnp.int32)
    slots = slots.transpose(1, 0, 2).reshape(-1).astype(jnp.int32)
    return (owners, slots)


def draw_dest_owner(key, part):
    return route_plan(key)[0]


def draw_dest_slot(key, part):
    return route_plan(key)[1]


def spiked(result, rng, source, target, shards_of, factor):
    def block_of(axis_at):
        return (jnp.arange(result.shape[axis_at]) // (result.shape[axis_at] // shards_of)).reshape((-1,) + (1,) * (result.ndim - 1 - axis_at))

    one_side = jax.random.permutation(rng, shards_of)[block_of(target)]
    far = (block_of(target) + shards_of // 2) % shards_of
    return jnp.where((block_of(source) == one_side) | (block_of(source) == far), factor * result, result)


def levels(rng, extent, pieces, smallest, largest):
    loudness, own = 1.0, jax.random.fold_in(rng, 6)
    for dim, blocks in pieces:
        steps = jnp.exp(jax.random.uniform(jax.random.fold_in(own, dim), (blocks,), jnp.float32, smallest / len(pieces), largest / len(pieces)))
        loudness = loudness * jnp.repeat(steps, extent[dim] // blocks).reshape([-1 if axis == dim else 1 for axis in range(len(extent))])
    return loudness


def split_up(amount, total, bound, skew):
    loads = [(1 << 20) // math.isqrt(standing ** skew) + 1 for standing in range(2, amount + 1)]
    spare, given = total - bound - (amount - 1), [1] * (amount - 1)
    while spare > 0:
        free = [i for i in range(amount - 1) if given[i] < bound]
        mass, left = sum([loads[i] for i in free]), spare
        for i in free:
            addition = min(bound - given[i], max(1, left * loads[i] // mass), spare)
            given[i] = given[i] + addition
            spare = spare - addition
    return np.array([bound] + given)


def ragged(own_key, amount, total, bound, slope):
    if amount == 2:
        one = jax.random.randint(own_key, (), max(1, total - bound), min(bound, total - 1) + 1)
        return jnp.stack([one, total - one])
    sizes = jnp.asarray(split_up(amount, total, bound, slope), jnp.int32)
    twos = (amount - 1) // 2
    donor, sink = sizes[1:1 + 2 * twos:2], sizes[2:2 + 2 * twos:2]
    room = jnp.minimum(donor - 1, bound - sink)
    passed = jax.random.randint(jax.random.fold_in(own_key, 1), (twos,), 0, 1 << 20) % (room + 1)
    sizes = sizes.at[1:1 + 2 * twos:2].set(donor - passed).at[2:2 + 2 * twos:2].set(sink + passed)
    return sizes[jax.random.permutation(jax.random.fold_in(own_key, 2), amount)]


def centred(key, dims, scale, reach, shards=(), held_as=jnp.bfloat16):
    gain = levels(key, dims, shards, -0.22, 0.18) if shards else 1.0
    drawn = jax.random.normal(key, dims, jnp.float32) * scale * gain
    return jnp.minimum(jnp.maximum(drawn, -reach), reach).astype(held_as)


def gaussian_with(stream_key, extent, scale, most, cuts, heavy, held_as=jnp.bfloat16):
    drawn = scale * jax.random.normal(stream_key, extent, jnp.float32)
    if cuts:
        drawn = drawn * levels(stream_key, extent, cuts, -0.22, 0.18)
    return jnp.clip(spiked(drawn, jax.random.fold_in(stream_key, 3), *heavy), -most, most).astype(held_as)


def setup_inputs(seed: int = 0) -> dict:
    seeds = jax.random.split(jax.random.key(seed), 11)
    features = gaussian_with(seeds[0], (EVENTS, D), 1.0, 24.0, ((0, 256),), (0, 1, 256, 6.0))
    dest_owner = draw_dest_owner(jax.random.fold_in(seeds[10], 71), 0)
    dest_slot = draw_dest_slot(jax.random.fold_in(seeds[10], 71), 0)
    doc_ids = jax.vmap(lambda own: jnp.searchsorted(jnp.cumsum(ragged(own, DOCS, LEN, DOC_MOST, 1)), jnp.arange(LEN), side="right"))(jax.random.split(seeds[3], SEQS)).reshape((SEQS, LEN)).astype(jnp.int32)
    enc_weight = centred(seeds[4], (ENC_LAYERS, D, D), D ** -0.5, 0.1875)
    attn_in = centred(seeds[5], (4, D, D), D ** -0.5, 0.1875, ((2, 4),))
    attn_out = centred(seeds[6], (D, D), D ** -0.5, 0.1875, ((0, 4),))
    ffn_in = centred(seeds[7], (2, D, FF), D ** -0.5, 0.1875, ((2, 4),))
    ffn_out = centred(seeds[8], (FF, D), FF ** -0.5, 0.125, ((0, 4),))
    out_grad = centred(seeds[9], (SEQS, LEN, D), 1.0, 6.0, ((0, 64), (1, 4)))
    return {"features": features, "dest_owner": dest_owner, "dest_slot": dest_slot, "doc_ids": doc_ids, "enc_weight": enc_weight, "attn_in": attn_in, "attn_out": attn_out, "ffn_in": ffn_in, "ffn_out": ffn_out, "out_grad": out_grad}


EPS = 1e-06

def silu_grad(value):
    sigma = jax.nn.sigmoid(value)
    return sigma * (1.0 + value * (1.0 - sigma))

def norm_rows(rows):
    wide = rows.astype(jnp.float32)
    factor = lax.rsqrt(lax.optimization_barrier(jnp.mean(wide * wide, axis=-1, keepdims=True)) + EPS)
    return (wide * factor, factor)

def norm_back(grad, normed, factor):
    return factor * (grad - normed * lax.optimization_barrier(jnp.mean(grad * normed, axis=-1, keepdims=True)))

def rounded(value):
    return lax.optimization_barrier(value.astype(jnp.bfloat16)).astype(jnp.float32)

def doc_counts(documents):
    length = documents.shape[0]
    places = jnp.arange(length, dtype=jnp.int32)
    change = jnp.concatenate([jnp.ones((1,), bool), documents[1:] != documents[:-1]])
    first = lax.cummax(jnp.where(change, places, 0), axis=0)
    return (places - first + 1).astype(jnp.float32)

def group_terms(left, right, spec):
    group_width = left.shape[-1] // N_TENSOR
    total = None
    for group in range(N_TENSOR):
        lower = group * group_width
        term = jnp.einsum(spec, left[..., lower:lower + group_width].astype(jnp.float32), right[..., lower:lower + group_width].astype(jnp.float32))
        total = rounded(term) if total is None else total + rounded(term)
    return total

def split_heads(value):
    return value.reshape(value.shape[0], HEADS, D // HEADS).transpose(1, 0, 2)

def join_heads(value):
    return value.transpose(1, 0, 2).reshape(value.shape[1], D)

def sequence_step(packed, documents, d_out, attn_in, attn_out, ffn_in, ffn_out):
    head_scale = (D // HEADS) ** (-0.5)
    counts = doc_counts(documents)
    root = jnp.sqrt(counts)[:, None]
    places = jnp.arange(LEN, dtype=jnp.int32)
    allowed = (documents[:, None] == documents[None, :]) & (places[None, :] <= places[:, None])
    normed_f, factor1 = norm_rows(packed)
    normed = normed_f.astype(jnp.bfloat16)
    projected = jnp.einsum('rd,kdc->krc', normed.astype(jnp.float32), attn_in.astype(jnp.float32)).astype(jnp.bfloat16)
    query = split_heads(projected[0]).astype(jnp.float32)
    keys = split_heads(projected[1]).astype(jnp.float32)
    values = split_heads(projected[2]).astype(jnp.float32)
    gate_raw = projected[3].astype(jnp.float32)
    scores = jnp.einsum('hqd,hkd->hqk', query, keys) * head_scale
    weights = jnp.where(allowed[None], jax.nn.silu(scores), 0.0).astype(jnp.bfloat16)
    attended = join_heads(jnp.einsum('hqk,hkd->hqd', weights.astype(jnp.float32), values)) / root
    gated = (attended * jax.nn.silu(gate_raw)).astype(jnp.bfloat16)
    attn_sum = group_terms(gated, attn_out.T, 'rc,dc->rd')
    resid = (packed.astype(jnp.float32) + attn_sum).astype(jnp.bfloat16)
    normed2_f, factor2 = norm_rows(resid)
    normed2 = normed2_f.astype(jnp.bfloat16)
    gate_up = jnp.einsum('rd,kdf->krf', normed2.astype(jnp.float32), ffn_in.astype(jnp.float32))
    gate, upper = (gate_up[0], gate_up[1])
    hidden = (jax.nn.silu(gate) * upper).astype(jnp.bfloat16)
    ffn_sum = group_terms(hidden, ffn_out.T, 'rf,df->rd')
    packed_out = (resid.astype(jnp.float32) + ffn_sum).astype(jnp.bfloat16)
    d_hidden = jnp.dot(d_out, ffn_out.T, preferred_element_type=jnp.float32)
    d_gate = (d_hidden * upper * silu_grad(gate)).astype(jnp.bfloat16)
    d_upper = (d_hidden * jax.nn.silu(gate)).astype(jnp.bfloat16)
    d_normed2 = group_terms(jnp.stack([d_gate, d_upper]), ffn_in, 'krf,kdf->rd')
    d_resid = (d_out.astype(jnp.float32) + norm_back(d_normed2, normed2_f, factor2)).astype(jnp.bfloat16)
    d_gated = jnp.dot(d_resid, attn_out.T, preferred_element_type=jnp.float32)
    d_attended = (d_gated * jax.nn.silu(gate_raw) / root).astype(jnp.bfloat16)
    d_gate_proj = (d_gated * attended * silu_grad(gate_raw)).astype(jnp.bfloat16)
    d_att_heads = split_heads(d_attended).astype(jnp.float32)
    d_weights = jnp.einsum('hqd,hkd->hqk', d_att_heads, values)
    d_scores = jnp.where(allowed[None], d_weights * silu_grad(scores), 0.0).astype(jnp.bfloat16).astype(jnp.float32)
    d_query = (jnp.einsum('hqk,hkd->hqd', d_scores, keys) * head_scale).astype(jnp.bfloat16)
    d_keys = (jnp.einsum('hqk,hqd->hkd', d_scores, query) * head_scale).astype(jnp.bfloat16)
    d_values = jnp.einsum('hqk,hqd->hkd', weights.astype(jnp.float32), d_att_heads).astype(jnp.bfloat16)
    d_projected = jnp.stack([join_heads(d_query), join_heads(d_keys), join_heads(d_values), d_gate_proj])
    d_normed = group_terms(d_projected, attn_in, 'krc,kdc->rd')
    d_packed = (d_resid.astype(jnp.float32) + norm_back(d_normed, normed_f, factor1)).astype(jnp.bfloat16)
    return (packed_out, d_packed)

def reference(features, dest_owner, dest_slot, doc_ids, enc_weight, attn_in, attn_out, ffn_in, ffn_out, out_grad):
    activations = [features]
    pre_acts = []
    for layer in range(ENC_LAYERS - 1):
        preact = jnp.dot(activations[-1], enc_weight[layer], preferred_element_type=jnp.float32)
        pre_acts.append(preact)
        activations.append(jax.nn.silu(preact).astype(jnp.bfloat16))
    encoded = jnp.dot(activations[-1], enc_weight[ENC_LAYERS - 1], preferred_element_type=jnp.float32).astype(jnp.bfloat16)
    device_of = jnp.arange(EVENTS, dtype=jnp.int32) // ROWS_DEV
    position = device_of % N_TENSOR * ROWS_DEV + dest_slot
    packed = jnp.zeros((SEQS, LEN, D), jnp.bfloat16).at[dest_owner, position].set(encoded)

    def one_sequence(inputs):
        return sequence_step(inputs[0], inputs[1], inputs[2], attn_in, attn_out, ffn_in, ffn_out)
    packed_out, d_packed = lax.map(one_sequence, (packed, doc_ids, out_grad))
    row_grad = d_packed[dest_owner, position]
    cotangent = row_grad
    grads = []
    for layer in reversed(range(ENC_LAYERS)):
        grads.append(lax.dot_general(activations[layer], cotangent, (((0,), (0,)), ((), ())), preferred_element_type=jnp.float32))
        if layer > 0:
            back = lax.dot_general(cotangent, enc_weight[layer], (((1,), (1,)), ((), ())), preferred_element_type=jnp.float32)
            cotangent = (back * silu_grad(pre_acts[layer - 1])).astype(jnp.bfloat16)
    enc_grad = jnp.stack(grads[::-1])
    return (packed_out, row_grad, enc_grad)
```

```python
import jax
import jax.numpy as jnp
from jax import lax
from jax.experimental import pallas as pl
from jax.experimental.pallas import tpu as pltpu
from jax.sharding import PartitionSpec as P

D = 1024
HEADS = 16


EPS = 1e-06
BLOCK = 256


def joined_along(blocks, dim):
    blocks = jnp.moveaxis(blocks, 0, dim)
    lengths = blocks.shape
    return blocks.reshape(*lengths[:dim], lengths[dim] * lengths[dim + 1], *lengths[dim + 2 :])


def sent_to_all(array, axis):
    copies = jnp.broadcast_to(array, (lax.axis_size(axis), *array.shape))
    return lax.all_to_all(copies, axis, split_axis=0, concat_axis=0, tiled=True)


def gather_directly(array, axis, dim):
    return joined_along(sent_to_all(array, axis), dim)


def cut_along(array, dim, length):
    lengths = array.shape
    blocks = array.reshape(*lengths[:dim], length, lengths[dim] // length, *lengths[dim + 1 :])
    return jnp.moveaxis(blocks, dim, 0)


def sent_and_summed(array, axis, dim):
    blocks = cut_along(array, dim, lax.axis_size(axis))
    arrived = lax.all_to_all(blocks, axis, split_axis=0, concat_axis=0, tiled=True)
    return arrived.astype(jnp.float32).sum(axis=0)


def silu_grad(value):
    sigma = jax.nn.sigmoid(value)
    return sigma * (1.0 + value * (1.0 - sigma))


def norm_rows(rows):
    wide = rows.astype(jnp.float32)
    factor = lax.rsqrt(jnp.mean(wide * wide, axis=-1, keepdims=True) + EPS)
    return (wide * factor, factor)


def norm_back(grad, normed, factor):
    return factor * (grad - normed * jnp.mean(grad * normed, axis=-1, keepdims=True))


def rounded(value):
    return lax.optimization_barrier(value.astype(jnp.bfloat16)).astype(jnp.float32)


def doc_counts(documents):
    length = documents.shape[0]
    places = jnp.arange(length, dtype=jnp.int32)
    change = jnp.concatenate([jnp.ones((1,), bool), documents[1:] != documents[:-1]])
    first = lax.cummax(jnp.where(change, places, 0), axis=0)
    return (places - first + 1).astype(jnp.float32)


def tile_mask(documents, q_start, k_start, q_len, k_len):
    q_docs = documents[q_start : q_start + q_len]
    k_docs = documents[k_start : k_start + k_len]
    q_place = q_start + jnp.arange(q_len, dtype=jnp.int32)
    k_place = k_start + jnp.arange(k_len, dtype=jnp.int32)
    return (q_docs[:, None] == k_docs[None, :]) & (k_place[None, :] <= q_place[:, None])


def tile_forward(query, keys, values, allowed):
    scores = jnp.einsum(
        "hqd,hkd->hqk", query, keys, preferred_element_type=jnp.float32
    ) * query.shape[-1] ** (-0.5)
    weights = jnp.where(allowed[None], jax.nn.silu(scores), 0.0).astype(jnp.bfloat16)
    return jnp.einsum("hqk,hkd->hqd", weights, values, preferred_element_type=jnp.float32)


def tile_backward(query, keys, values, d_attended, allowed):
    head_scale = query.shape[-1] ** (-0.5)
    scores = (
        jnp.einsum("hqd,hkd->hqk", query, keys, preferred_element_type=jnp.float32) * head_scale
    )
    weights = jnp.where(allowed[None], jax.nn.silu(scores), 0.0).astype(jnp.bfloat16)
    d_weights = jnp.einsum("hqd,hkd->hqk", d_attended, values, preferred_element_type=jnp.float32)
    d_scores = jnp.where(allowed[None], d_weights * silu_grad(scores), 0.0).astype(jnp.bfloat16)
    d_query = (
        jnp.einsum("hqk,hkd->hqd", d_scores, keys, preferred_element_type=jnp.float32) * head_scale
    )
    d_keys = (
        jnp.einsum("hqk,hqd->hkd", d_scores, query, preferred_element_type=jnp.float32) * head_scale
    )
    d_values = jnp.einsum("hqk,hqd->hkd", weights, d_attended, preferred_element_type=jnp.float32)
    return (d_query, d_keys, d_values)


def attend(query, keys, values, documents):
    length = query.shape[1]
    block = min(BLOCK, length)
    outputs = []
    for q_index in range(length // block):
        q_start = q_index * block
        query_block = query[:, q_start : q_start + block]
        limit = q_start + block
        allowed = tile_mask(documents, q_start, 0, block, limit)
        outputs.append(tile_forward(query_block, keys[:, :limit], values[:, :limit], allowed))
    return jnp.concatenate(outputs, axis=1)


def attend_back(query, keys, values, d_attended, documents):
    length = query.shape[1]
    block = min(BLOCK, length)
    d_query_parts = []
    d_keys = jnp.zeros(keys.shape, jnp.float32)
    d_values = jnp.zeros(values.shape, jnp.float32)
    for q_index in range(length // block):
        q_start = q_index * block
        query_block = query[:, q_start : q_start + block]
        d_att_block = d_attended[:, q_start : q_start + block]
        limit = q_start + block
        allowed = tile_mask(documents, q_start, 0, block, limit)
        part_q, part_k, part_v = tile_backward(
            query_block, keys[:, :limit], values[:, :limit], d_att_block, allowed
        )
        d_query_parts.append(part_q)
        d_keys = d_keys.at[:, :limit].add(part_k)
        d_values = d_values.at[:, :limit].add(part_v)
    return (jnp.concatenate(d_query_parts, axis=1), d_keys, d_values)


MESH = pl.DeviceIdType.MESH
GROUPS = 64
CAP = 3
BLOCK_ROWS = CAP * 8
VMEM_LIMIT = 60 * 1024 * 1024


def where_am_i():
    return (lax.axis_index("event"), lax.axis_index("pack"), lax.axis_index("tensor"))


def peer(index, tensor):
    return (index // 8, lax.rem(index, 8), tensor)


def greet_all(barrier, me, tensor):
    def greet(step, carry):
        pl.semaphore_signal(
            barrier, inc=1, device_id=peer(lax.rem(me + step, GROUPS), tensor), device_id_type=MESH
        )
        return carry

    lax.fori_loop(1, GROUPS, greet, 0)


def exchange_copy(source, target, me, tensor, step, send_sem, recv_sem):
    other = lax.rem(me + step, GROUPS)
    return pltpu.make_async_remote_copy(
        src_ref=source.at[other],
        dst_ref=target.at[me],
        send_sem=send_sem,
        recv_sem=recv_sem,
        device_id=peer(other, tensor),
        device_id_type=MESH,
    )


def start_exchange(source, target, me, tensor, send_sem, recv_sem):
    def start(step, carry):
        exchange_copy(source, target, me, tensor, step, send_sem, recv_sem).start()
        return carry

    lax.fori_loop(1, GROUPS, start, 0)
    target[me] = source[me]


def await_bytes(ref, sem):
    pltpu.make_async_copy(ref, ref, sem).wait()


def end_exchange(source, target, send_sem, recv_sem):
    await_bytes(source.at[pl.ds(0, GROUPS - 1)], send_sem)
    await_bytes(target.at[pl.ds(0, GROUPS - 1)], recv_sem)


def dot32(left, right, dims=((1,), (0,))):
    return lax.dot_general(left, right, (dims, ((), ())), preferred_element_type=jnp.float32)


def routing(owner_row):
    rows = jnp.broadcast_to(owner_row, (128, 128))
    columns = rows.T
    earlier = lax.broadcasted_iota(jnp.int32, (128, 128), 0) < lax.broadcasted_iota(
        jnp.int32, (128, 128), 1
    )
    rank = jnp.sum(jnp.where((columns == rows) & earlier, 1.0, 0.0), axis=0, keepdims=True)
    group = lax.broadcasted_iota(jnp.int32, (GROUPS, 128), 0).astype(jnp.float32)
    mine = owner_row == group
    return [mine & (rank == float(k)) for k in range(CAP)]


def one_hot(mask):
    return jnp.where(mask, 1.0, 0.0).astype(jnp.bfloat16)


def spread_rows(wide, k, rows):
    for part in range(8):
        wide[pl.ds(k * 8 + part, GROUPS, stride=BLOCK_ROWS), :] = rows[
            :, part * 128 : (part + 1) * 128
        ]


def joined_rows(wide, k):
    return jnp.concatenate(
        [wide[pl.ds(k * 8 + part, GROUPS, stride=BLOCK_ROWS), :] for part in range(8)], axis=1
    ).astype(jnp.bfloat16)


def silu(value):
    return value * jax.nn.sigmoid(value)


def dispatch_kernel(
    features,
    owner,
    slot,
    weight_hbm,
    quarter,
    preact,
    activation,
    got_slots,
    weight,
    wide,
    send_rows,
    got_rows,
    send_slots,
    load_sem,
    send_sem,
    recv_sem,
):
    event, pack, tensor = where_am_i()
    me = event * 8 + pack
    barrier = pltpu.get_barrier_semaphore()
    loads = []
    for layer in range(2):
        load = pltpu.make_async_copy(weight_hbm.at[layer], weight.at[layer], load_sem.at[layer])
        load.start()
        loads.append(load)
    greet_all(barrier, me, tensor)
    picks = routing(owner[...].astype(jnp.float32))
    slot_row = slot[...].astype(jnp.float32) + 1.0
    lane = lax.broadcasted_iota(jnp.int32, (GROUPS, 128), 1)
    slots = jnp.full((GROUPS, 128), -1.0, jnp.float32)
    for k in range(CAP):
        value = jnp.sum(jnp.where(picks[k], slot_row, 0.0), axis=1, keepdims=True) - 1.0
        slots = jnp.where(lane == k, value, slots)
    send_slots[:, 0, :] = slots
    loads[0].wait()
    pre = dot32(features[...], weight[0])
    preact[...] = pre
    act = silu(pre).astype(jnp.bfloat16)
    activation[...] = act
    loads[1].wait()
    encoded = dot32(act, weight[1]).astype(jnp.bfloat16)
    for k in range(CAP):
        spread_rows(wide, k, dot32(one_hot(picks[k]), encoded))
    send_rows[...] = wide[...].astype(jnp.bfloat16).reshape(GROUPS, BLOCK_ROWS, 128)
    pl.semaphore_wait(barrier, GROUPS - 1)
    start_exchange(send_slots, got_slots, me, tensor, send_sem.at[0], recv_sem.at[0])
    start_exchange(send_rows, got_rows, me, tensor, send_sem.at[1], recv_sem.at[1])
    end_exchange(send_slots, got_slots, send_sem.at[0], recv_sem.at[0])
    end_exchange(send_rows, got_rows, send_sem.at[1], recv_sem.at[1])
    wide[...] = got_rows[...].reshape(GROUPS * BLOCK_ROWS, 128).astype(jnp.float32)
    turned = jnp.concatenate(
        [got_slots[:, 0, :], jnp.full((GROUPS, 128), -1.0, jnp.float32)], axis=0
    ).T
    place = lax.broadcasted_iota(jnp.int32, (128, GROUPS), 0).astype(jnp.float32)
    total = None
    for k in range(CAP):
        pick = one_hot(turned[k : k + 1, :GROUPS] == place)
        term = dot32(pick, joined_rows(wide, k))
        total = term if total is None else total + term
    quarter[...] = total.astype(jnp.bfloat16)


def dispatch(features, owner, slot, enc_weight):
    vmem = pl.BlockSpec(memory_space=pltpu.VMEM)
    return pl.pallas_call(
        dispatch_kernel,
        out_shape=(
            jax.ShapeDtypeStruct((128, 1024), jnp.bfloat16),
            jax.ShapeDtypeStruct((128, 1024), jnp.float32),
            jax.ShapeDtypeStruct((128, 1024), jnp.bfloat16),
            jax.ShapeDtypeStruct((GROUPS, 1, 128), jnp.float32),
        ),
        in_specs=[vmem, vmem, vmem, pl.BlockSpec(memory_space=pl.ANY)],
        out_specs=(vmem, vmem, vmem, vmem),
        scratch_shapes=[
            pltpu.VMEM((2, 1024, 1024), jnp.bfloat16),
            pltpu.VMEM((GROUPS * BLOCK_ROWS, 128), jnp.float32),
            pltpu.VMEM((GROUPS, BLOCK_ROWS, 128), jnp.bfloat16),
            pltpu.VMEM((GROUPS, BLOCK_ROWS, 128), jnp.bfloat16),
            pltpu.VMEM((GROUPS, 1, 128), jnp.float32),
            pltpu.SemaphoreType.DMA((2,)),
            pltpu.SemaphoreType.DMA((2,)),
            pltpu.SemaphoreType.DMA((2,)),
        ],
        compiler_params=pltpu.CompilerParams(
            collective_id=0, has_side_effects=True, vmem_limit_bytes=VMEM_LIMIT
        ),
        name="dispatch",
    )(features, owner.reshape(1, 128), slot.reshape(1, 128), enc_weight)


class Halving:
    def __init__(self, blocks, first, second, outgoing, sems, base, index, device):
        self.blocks, self.first, self.second, self.outgoing = blocks, first, second, outgoing
        self.sems, self.base, self.index = sems, base, index
        near = index + 1 - 2 * lax.rem(index, 2)
        self.other = (near, 3 - index)
        self.far = lax.rem(index + 2, 4)
        self.device = device

    def copy(self, source, target, number, half_partner):
        send, recv = self.sems
        return pltpu.make_async_remote_copy(
            src_ref=source,
            dst_ref=target,
            send_sem=send.at[self.base + number],
            recv_sem=recv.at[self.base + number],
            device_id=self.device(half_partner),
            device_id_type=MESH,
        )

    def round_one(self):
        copies = []
        for half in range(2):
            partner = self.other[half]
            for slot, block in enumerate((partner, self.far)):
                copies.append(
                    self.copy(
                        self.blocks.at[block, half],
                        self.first.at[half, slot],
                        half * 2 + slot,
                        partner,
                    )
                )
        return copies

    def round_two(self):
        return [
            self.copy(self.outgoing.at[half], self.second.at[half], 4 + half, self.other[1 - half])
            for half in range(2)
        ]

    def start_one(self):
        for copy in self.round_one():
            copy.start()

    def start_two(self):
        for copy in self.round_one():
            copy.wait()
        for half in range(2):
            block = self.other[1 - half]
            self.outgoing[half] = (
                self.blocks[block, half].astype(jnp.float32)
                + self.first[half, 1].astype(jnp.float32)
            ).astype(jnp.bfloat16)
        for copy in self.round_two():
            copy.start()

    def finish(self):
        for copy in self.round_two():
            copy.wait()
        return [
            (
                self.blocks[self.index, half].astype(jnp.float32)
                + self.first[half, 0].astype(jnp.float32)
                + self.second[half].astype(jnp.float32)
            ).astype(jnp.bfloat16)
            for half in range(2)
        ]


def back_kernel(
    d_quarter,
    got_slots,
    owner,
    features,
    activation,
    preact,
    weight_hbm,
    row_grad,
    enc_grad,
    weight,
    wide,
    send_rows,
    got_rows,
    acts,
    cots,
    grads,
    firsts,
    seconds,
    outs,
    grads2,
    firsts2,
    seconds2,
    outs2,
    send_z,
    got_z,
    load_sem,
    send_sem,
    recv_sem,
    pair_send,
    pair_recv,
    half_send,
    half_recv,
    z_send,
    z_recv,
):
    event, pack, tensor = where_am_i()
    me = event * 8 + pack
    core = lax.rem(event, 2)
    chip_x = event // 2
    partner = (event + 1 - 2 * core, pack, tensor)
    barrier = pltpu.get_barrier_semaphore()
    load = pltpu.make_async_copy(weight_hbm.at[1], weight, load_sem.at[0])
    load.start()
    greet_all(barrier, me, tensor)
    for shift in (1, 3):
        pl.semaphore_signal(
            barrier,
            inc=1,
            device_id=(event, pack, lax.rem(tensor + shift, 4)),
            device_id_type=MESH,
        )

    def pair_copy(number, array):
        return pltpu.make_async_remote_copy(
            src_ref=array.at[0],
            dst_ref=array.at[1],
            send_sem=pair_send.at[number],
            recv_sem=pair_recv.at[number],
            device_id=partner,
            device_id_type=MESH,
        )

    acts[0, 0] = features[...]
    acts[1, 0] = activation[...]
    lane = lax.broadcasted_iota(jnp.int32, (GROUPS, 128), 1).astype(jnp.float32)
    for k in range(CAP):
        pick = one_hot(got_slots[:, 0, k : k + 1] == lane)
        spread_rows(wide, k, dot32(pick, d_quarter[...]))
    send_rows[...] = wide[...].astype(jnp.bfloat16).reshape(GROUPS, BLOCK_ROWS, 128)
    pl.semaphore_wait(barrier, GROUPS - 1 + 2)
    start_exchange(send_rows, got_rows, me, tensor, send_sem.at[0], recv_sem.at[0])
    act_copies = [pair_copy(layer, acts.at[layer]) for layer in range(2)]
    for copy in act_copies:
        copy.start()
    picks = routing(owner[...].astype(jnp.float32))
    load.wait()
    for copy in act_copies:
        copy.wait()
    end_exchange(send_rows, got_rows, send_sem.at[0], recv_sem.at[0])
    wide[...] = got_rows[...].reshape(GROUPS * BLOCK_ROWS, 128).astype(jnp.float32)
    total = None
    for k in range(CAP):
        term = dot32(one_hot(picks[k]), joined_rows(wide, k), ((0,), (0,)))
        total = term if total is None else total + term
    cotangent = total.astype(jnp.bfloat16)
    row_grad[...] = cotangent
    cots[1, 0] = cotangent
    cot_copies = [pair_copy(2 + layer, cots.at[layer]) for layer in range(2)]
    cot_copies[1].start()
    pre = preact[...]
    sigma = jax.nn.sigmoid(pre)
    back = dot32(cotangent, weight[...], ((1,), (1,)))
    cots[0, 0] = (back * (sigma * (1.0 + pre * (1.0 - sigma)))).astype(jnp.bfloat16)
    cot_copies[0].start()

    def tensor_device(index):
        return (event, pack, index)

    def chip_device(index):
        return (index * 2 + core, pack, tensor)

    rings = ((chip_x, chip_device), (tensor, tensor_device))
    stages = [[], []]
    for layer in range(2):
        for stage, refs in enumerate(
            ((grads, firsts, seconds, outs), (grads2, firsts2, seconds2, outs2))
        ):
            index, device = rings[layer] if stage == 0 else rings[1 - layer]
            stages[stage].append(
                Halving(
                    *(ref.at[layer] for ref in refs),
                    (half_send, half_recv),
                    (stage * 2 + layer) * 6,
                    index,
                    device,
                )
            )
    for layer in (1, 0):
        cot_copies[layer].wait()
        cot = cots[layer].reshape(256, 1024)
        for chip in range(4):
            columns = pl.ds(pl.multiple_of((chip * 2 + core) * 128, 128), 128)
            act = acts[layer, :, :, columns].reshape(256, 128)
            term = dot32(act, cot, ((0,), (0,))).astype(jnp.bfloat16)
            for block in range(4):
                for half in range(2):
                    piece = term[half * 64 : (half + 1) * 64, block * 256 : (block + 1) * 256]
                    if layer == 1:
                        grads[layer, block, half, chip] = piece
                    else:
                        grads[layer, chip, half, block] = piece
        stages[0][layer].start_one()
    for layer in (1, 0):
        stages[0][layer].start_two()
    for layer in (1, 0):
        for half, value in enumerate(stages[0][layer].finish()):
            for block in range(4):
                grads2[layer, block, half] = value[block]
        stages[1][layer].start_one()
    for layer in (1, 0):
        stages[1][layer].start_two()
    for layer in (1, 0):
        for half, value in enumerate(stages[1][layer].finish()):
            for quarter in range(4):
                send_z[half * 4 + quarter, layer] = value[quarter * 16 : (quarter + 1) * 16]
    z_copies = []
    for step in (1, 7, 2, 6, 3, 5, 4):
        other = lax.rem(pack + step, 8)
        z_copies.append(
            pltpu.make_async_remote_copy(
                src_ref=send_z.at[other],
                dst_ref=got_z.at[pack],
                send_sem=z_send.at[step],
                recv_sem=z_recv.at[step],
                device_id=(event, other, tensor),
                device_id_type=MESH,
            )
        )
        z_copies[-1].start()
    got_z[pack] = send_z[pack]
    for copy in z_copies:
        copy.wait()
    total = got_z[0].astype(jnp.float32)
    for source in range(1, 8):
        total = total + got_z[source].astype(jnp.float32)
    enc_grad[...] = total


def give_back(d_quarter, got_slots, owner, features, activation, preact, enc_weight):
    vmem = pl.BlockSpec(memory_space=pltpu.VMEM)
    bf16 = jnp.bfloat16
    return pl.pallas_call(
        back_kernel,
        out_shape=(
            jax.ShapeDtypeStruct((128, 1024), bf16),
            jax.ShapeDtypeStruct((2, 16, 256), jnp.float32),
        ),
        in_specs=[vmem] * 6 + [pl.BlockSpec(memory_space=pl.ANY)],
        out_specs=(vmem, vmem),
        scratch_shapes=[
            pltpu.VMEM((1024, 1024), bf16),
            pltpu.VMEM((GROUPS * BLOCK_ROWS, 128), jnp.float32),
            pltpu.VMEM((GROUPS, BLOCK_ROWS, 128), bf16),
            pltpu.VMEM((GROUPS, BLOCK_ROWS, 128), bf16),
            pltpu.VMEM((2, 2, 128, 1024), bf16),
            pltpu.VMEM((2, 2, 128, 1024), bf16),
            pltpu.VMEM((2, 4, 2, 4, 64, 256), bf16),
            pltpu.VMEM((2, 2, 2, 4, 64, 256), bf16),
            pltpu.VMEM((2, 2, 4, 64, 256), bf16),
            pltpu.VMEM((2, 2, 4, 64, 256), bf16),
            pltpu.VMEM((2, 4, 2, 64, 256), bf16),
            pltpu.VMEM((2, 2, 2, 64, 256), bf16),
            pltpu.VMEM((2, 2, 64, 256), bf16),
            pltpu.VMEM((2, 2, 64, 256), bf16),
            pltpu.VMEM((8, 2, 16, 256), bf16),
            pltpu.VMEM((8, 2, 16, 256), bf16),
            pltpu.SemaphoreType.DMA((1,)),
            pltpu.SemaphoreType.DMA((1,)),
            pltpu.SemaphoreType.DMA((1,)),
            pltpu.SemaphoreType.DMA((4,)),
            pltpu.SemaphoreType.DMA((4,)),
            pltpu.SemaphoreType.DMA((24,)),
            pltpu.SemaphoreType.DMA((24,)),
            pltpu.SemaphoreType.DMA((8,)),
            pltpu.SemaphoreType.DMA((8,)),
        ],
        compiler_params=pltpu.CompilerParams(
            collective_id=1, has_side_effects=True, vmem_limit_bytes=VMEM_LIMIT
        ),
        name="give_back",
    )(d_quarter, got_slots, owner.reshape(1, 128), features, activation, preact, enc_weight)


def shards(
    features,
    dest_owner,
    dest_slot,
    doc_ids,
    enc_weight,
    attn_in,
    attn_out,
    ffn_in,
    ffn_out,
    out_grad,
):
    quarter, preact, activation, got_slots = dispatch(features, dest_owner, dest_slot, enc_weight)
    documents = doc_ids[0]
    root = jnp.sqrt(doc_counts(documents))[:, None]
    normed_f, factor1 = norm_rows(quarter)
    normed = normed_f.astype(jnp.bfloat16)
    projected = jnp.einsum(
        "rd,kdc->krc",
        gather_directly(normed, "tensor", 0),
        attn_in,
        preferred_element_type=jnp.float32,
    ).astype(jnp.bfloat16)
    length = projected.shape[1]
    local_cols = projected.shape[2]
    head_dim = D // HEADS
    local_heads = local_cols // head_dim

    def split_heads(value):
        return value.reshape(length, local_heads, head_dim).transpose(1, 0, 2)

    def join_heads(value):
        return value.transpose(1, 0, 2).reshape(length, local_cols)

    query = split_heads(projected[0])
    keys = split_heads(projected[1])
    values = split_heads(projected[2])
    gate_raw = projected[3].astype(jnp.float32)
    attended = join_heads(attend(query, keys, values, documents)) / root
    gated = (attended * jax.nn.silu(gate_raw)).astype(jnp.bfloat16)
    attn_sum = sent_and_summed(
        rounded(jnp.dot(gated, attn_out, preferred_element_type=jnp.float32)).astype(jnp.bfloat16),
        "tensor",
        0,
    )
    resid = (quarter.astype(jnp.float32) + attn_sum).astype(jnp.bfloat16)
    normed2_f, factor2 = norm_rows(resid)
    normed2 = normed2_f.astype(jnp.bfloat16)
    gate_up = jnp.einsum(
        "rd,kdf->krf",
        gather_directly(normed2, "tensor", 0),
        ffn_in,
        preferred_element_type=jnp.float32,
    )
    gate = gate_up[0]
    upper = gate_up[1]
    hidden = (jax.nn.silu(gate) * upper).astype(jnp.bfloat16)
    ffn_sum = sent_and_summed(
        rounded(jnp.dot(hidden, ffn_out, preferred_element_type=jnp.float32)).astype(jnp.bfloat16),
        "tensor",
        0,
    )
    packed_out = (resid.astype(jnp.float32) + ffn_sum).astype(jnp.bfloat16)
    d_out = out_grad[0]
    d_hidden = lax.dot_general(
        gather_directly(d_out, "tensor", 0),
        ffn_out,
        (((1,), (1,)), ((), ())),
        preferred_element_type=jnp.float32,
    )
    d_gate = (d_hidden * upper * silu_grad(gate)).astype(jnp.bfloat16)
    d_upper = (d_hidden * jax.nn.silu(gate)).astype(jnp.bfloat16)
    d_both = jnp.stack([d_gate, d_upper])
    piece = d_both
    d_normed2 = sent_and_summed(
        rounded(
            jnp.einsum("krf,kdf->rd", piece, ffn_in, preferred_element_type=jnp.float32)
        ).astype(jnp.bfloat16),
        "tensor",
        0,
    )
    d_resid = (d_out.astype(jnp.float32) + norm_back(d_normed2, normed2_f, factor2)).astype(
        jnp.bfloat16
    )
    d_gated = lax.dot_general(
        gather_directly(d_resid, "tensor", 0),
        attn_out,
        (((1,), (1,)), ((), ())),
        preferred_element_type=jnp.float32,
    )
    d_attended = (d_gated * jax.nn.silu(gate_raw) / root).astype(jnp.bfloat16)
    d_gate_proj = (d_gated * attended * silu_grad(gate_raw)).astype(jnp.bfloat16)
    d_query, d_keys, d_values = attend_back(query, keys, values, split_heads(d_attended), documents)
    d_projected = jnp.stack(
        [
            join_heads(d_query).astype(jnp.bfloat16),
            join_heads(d_keys).astype(jnp.bfloat16),
            join_heads(d_values).astype(jnp.bfloat16),
            d_gate_proj,
        ]
    )
    piece = d_projected
    d_normed = sent_and_summed(
        rounded(
            jnp.einsum("krc,kdc->rd", piece, attn_in, preferred_element_type=jnp.float32)
        ).astype(jnp.bfloat16),
        "tensor",
        0,
    )
    d_quarter = (d_resid.astype(jnp.float32) + norm_back(d_normed, normed_f, factor1)).astype(
        jnp.bfloat16
    )
    row_grad, enc_grad = give_back(
        d_quarter, got_slots, dest_owner, features, activation, preact, enc_weight
    )
    return (packed_out[None], row_grad, enc_grad)


def solution(mesh):
    placed = (
        P(("event", "pack", "tensor"), None),
        P(("event", "pack", "tensor")),
        P(("event", "pack", "tensor")),
        P(("event", "pack"), None),
        P(),
        P(None, None, "tensor"),
        P("tensor", None),
        P(None, None, "tensor"),
        P("tensor", None),
        P(("event", "pack"), "tensor", None),
    )
    return jax.shard_map(
        shards,
        mesh=mesh,
        in_specs=placed,
        out_specs=(
            P(("event", "pack"), "tensor", None),
            P(("event", "pack", "tensor"), None),
            P(None, ("event", "pack"), "tensor"),
        ),
        check_vma=False,
    )
```

```python
import jax
import jax.numpy as jnp
from jax import lax
from jax.experimental import pallas as pl
from jax.experimental.pallas import tpu as pltpu
from jax.sharding import PartitionSpec as P

MESH = pl.DeviceIdType.MESH
EPS = 1e-06
GROUPS = 64
CAP = 3
BLOCK_ROWS = CAP * 8
VMEM_LIMIT = 63 * 1024 * 1024
HEAD_SCALE = 64**-0.5


def silu_grad(value):
    sigma = jax.nn.sigmoid(value)
    return sigma * (1.0 + value * (1.0 - sigma))


def norm_rows(rows):
    factor = lax.rsqrt(jnp.mean(rows * rows, axis=-1, keepdims=True) + EPS)
    return (rows * factor, factor)


def norm_back(grad, normed, factor):
    return factor * (grad - normed * jnp.mean(grad * normed, axis=-1, keepdims=True))


def where_am_i():
    return (lax.axis_index("event"), lax.axis_index("pack"), lax.axis_index("tensor"))


def peer(index, tensor):
    return (index // 8, lax.rem(index, 8), tensor)


def greet_all(barrier, me, tensor):
    def greet(step, carry):
        pl.semaphore_signal(
            barrier, inc=1, device_id=peer(lax.rem(me + step, GROUPS), tensor), device_id_type=MESH
        )
        return carry

    lax.fori_loop(1, GROUPS, greet, 0)


def exchange_copy(source, target, me, tensor, step, send_sem, recv_sem):
    other = lax.rem(me + step, GROUPS)
    return pltpu.make_async_remote_copy(
        src_ref=source.at[other],
        dst_ref=target.at[me],
        send_sem=send_sem,
        recv_sem=recv_sem,
        device_id=peer(other, tensor),
        device_id_type=MESH,
    )


def start_exchange(source, target, me, tensor, send_sem, recv_sem):
    def start(step, carry):
        exchange_copy(source, target, me, tensor, step, send_sem, recv_sem).start()
        return carry

    lax.fori_loop(1, GROUPS, start, 0)
    target[me] = source[me]


def await_bytes(ref, sem):
    pltpu.make_async_copy(ref, ref, sem).wait()


def end_exchange(source, target, send_sem, recv_sem):
    await_bytes(source.at[pl.ds(0, GROUPS - 1)], send_sem)
    await_bytes(target.at[pl.ds(0, GROUPS - 1)], recv_sem)


def dot32(left, right, dims=((1,), (0,))):
    return lax.dot_general(left, right, (dims, ((), ())), preferred_element_type=jnp.float32)


def routing(owner_row):
    rows = jnp.broadcast_to(owner_row, (128, 128))
    columns = rows.T
    earlier = lax.broadcasted_iota(jnp.int32, (128, 128), 0) < lax.broadcasted_iota(
        jnp.int32, (128, 128), 1
    )
    rank = jnp.sum(jnp.where((columns == rows) & earlier, 1.0, 0.0), axis=0, keepdims=True)
    group = lax.broadcasted_iota(jnp.int32, (GROUPS, 128), 0).astype(jnp.float32)
    mine = owner_row == group
    return [mine & (rank == float(k)) for k in range(CAP)]


def one_hot(mask):
    return jnp.where(mask, 1.0, 0.0).astype(jnp.bfloat16)


def spread_rows(wide, k, rows):
    for part in range(8):
        wide[pl.ds(k * 8 + part, GROUPS, stride=BLOCK_ROWS), :] = rows[
            :, part * 128 : (part + 1) * 128
        ]


def joined_rows(wide, k):
    return jnp.concatenate(
        [wide[pl.ds(k * 8 + part, GROUPS, stride=BLOCK_ROWS), :] for part in range(8)], axis=1
    ).astype(jnp.bfloat16)


def silu(value):
    return value * jax.nn.sigmoid(value)


class Halving:
    def __init__(self, blocks, first, second, outgoing, sems, base, index, device):
        self.blocks, self.first, self.second, self.outgoing = blocks, first, second, outgoing
        self.sems, self.base, self.index = sems, base, index
        near = index + 1 - 2 * lax.rem(index, 2)
        self.other = (near, 3 - index)
        self.far = lax.rem(index + 2, 4)
        self.device = device

    def copy(self, source, target, number, half_partner):
        send, recv = self.sems
        return pltpu.make_async_remote_copy(
            src_ref=source,
            dst_ref=target,
            send_sem=send.at[self.base + number],
            recv_sem=recv.at[self.base + number],
            device_id=self.device(half_partner),
            device_id_type=MESH,
        )

    def round_one(self):
        copies = []
        for half in range(2):
            partner = self.other[half]
            for slot, block in enumerate((partner, self.far)):
                copies.append(
                    self.copy(
                        self.blocks.at[block, half],
                        self.first.at[half, slot],
                        half * 2 + slot,
                        partner,
                    )
                )
        return copies

    def round_two(self):
        return [
            self.copy(self.outgoing.at[half], self.second.at[half], 4 + half, self.other[1 - half])
            for half in range(2)
        ]

    def start_one(self):
        for copy in self.round_one():
            copy.start()

    def start_two(self):
        for copy in self.round_one():
            copy.wait()
        for half in range(2):
            block = self.other[1 - half]
            self.outgoing[half] = (
                self.blocks[block, half].astype(jnp.float32)
                + self.first[half, 1].astype(jnp.float32)
            ).astype(jnp.bfloat16)
        for copy in self.round_two():
            copy.start()

    def finish(self):
        for copy in self.round_two():
            copy.wait()
        return [
            (
                self.blocks[self.index, half].astype(jnp.float32)
                + self.first[half, 0].astype(jnp.float32)
                + self.second[half].astype(jnp.float32)
            ).astype(jnp.bfloat16)
            for half in range(2)
        ]


class Gather:
    def __init__(self, send, recv, event, pack, tensor):
        self.send, self.recv = send, recv
        self.event, self.pack, self.tensor = event, pack, tensor
        self.core = lax.rem(event, 2)
        self.used = 0
        self.started = []
        self.partner = (event + 1 - 2 * self.core, pack, tensor)
        self.pair_started = []

    def copy(self, source, target, device):
        number = self.used
        self.used += 1
        copy = pltpu.make_async_remote_copy(
            src_ref=source,
            dst_ref=target,
            send_sem=self.send.at[number],
            recv_sem=self.recv.at[number],
            device_id=device,
            device_id_type=MESH,
        )
        copy.start()
        self.started.append(copy)
        return copy

    def along_tensor(self, shift):
        return (self.event, self.pack, lax.rem(self.tensor + shift + 4, 4))

    def along_x(self, shift):
        return (lax.rem(self.event + 2 * shift + 8, 8), self.pack, self.tensor)

    def along_z(self, shift):
        return (self.event, lax.rem(self.pack + shift + 8, 8), self.tensor)

    def to_pair(self, region):
        self.pair_started.append(self.copy(region, region, self.partner))

    def end(self):
        for copy in self.started:
            copy.wait_send()
        for copy in self.pair_started:
            copy.wait_recv()


class TensorRing:
    def __init__(self, gather, own, region, halves):
        self.gather, self.own, self.region, self.halves = gather, own, region, halves

    def start(self):
        device = self.gather.along_tensor
        self.near = [
            self.gather.copy(self.own, self.region(2), device(1)),
            self.gather.copy(self.own, self.region(1), device(-1)),
        ]

    def relay(self):
        for copy in self.near:
            copy.wait_recv()
        device = self.gather.along_tensor
        plus, minus = self.halves
        self.far = [self.gather.copy(self.region(2, plus), self.region(3, plus), device(1))]
        if minus is not None:
            self.far.append(
                self.gather.copy(self.region(1, minus), self.region(3, minus), device(-1))
            )

    def end(self):
        for copy in self.far:
            copy.wait_recv()
        self.gather.to_pair(self.region(pl.ds(1, 3)))


class SideRing:
    def __init__(self, gather, size, index, device, region, halves):
        self.gather, self.size, self.index = gather, size, index
        self.device, self.region, self.halves = device, region, halves
        self.step = 0
        self.flying = None

    def block(self, shift, half=None):
        return self.region(lax.rem(self.index + shift + self.size, self.size), half)

    def start(self):
        block = self.block(0)
        self.flying = [
            self.gather.copy(block, block, self.device(1)),
            self.gather.copy(block, block, self.device(-1)),
        ]
        self.step = 1

    def advance(self):
        for copy in self.flying:
            copy.wait_recv()
        step = self.step
        last = step == self.size // 2
        forward = []
        if not last:
            halves = (None, None) if step + 1 < self.size // 2 else self.halves
            for sign, half in zip((1, -1), halves):
                if half is not False:
                    block = self.block(-sign * step, half)
                    forward.append(self.gather.copy(block, block, self.device(sign)))
            for sign in (1, -1):
                self.gather.to_pair(self.block(-sign * step))
        else:
            self.gather.to_pair(self.block(step))
        self.flying = forward
        self.step = step + 1


def masks(documents, tensor):
    own = documents[:, pl.ds(pl.multiple_of(tensor * 128, 128), 128)].astype(jnp.float32)
    before = documents[
        :, pl.ds(pl.multiple_of(lax.rem(tensor + 3, 4) * 128, 128), 128)
    ].astype(jnp.float32)
    before = before - jnp.where(tensor == 0, 1000.0, 0.0)
    mine = jnp.broadcast_to(own, (128, 128)).T
    row = lax.broadcasted_iota(jnp.int32, (128, 128), 0)
    column = lax.broadcasted_iota(jnp.int32, (128, 128), 1)
    allowed = jnp.concatenate(
        [
            jnp.where(mine == before, 1.0, 0.0),
            jnp.where((mine == own) & (column <= row), 1.0, 0.0),
        ],
        axis=1,
    )
    root = jnp.sqrt(jnp.sum(allowed, axis=1, keepdims=True))
    return (allowed, root)


def by_parity(value):
    first = lax.rem(lax.broadcasted_iota(jnp.int32, value.shape, 1), 128) < 64
    return (
        jnp.where(first, value, 0.0).astype(jnp.bfloat16),
        jnp.where(first, 0.0, value).astype(jnp.bfloat16),
    )


def rounded(value):
    return value.astype(jnp.bfloat16).astype(jnp.float32)


def step_kernel(
    features,
    owner,
    slot,
    documents,
    out_grad,
    enc_hbm,
    attn_in_hbm,
    attn_out_hbm,
    ffn_in_hbm,
    ffn_out_hbm,
    packed_out,
    row_grad,
    enc_grad,
    enc,
    attn_in,
    attn_out,
    ffn_in,
    ffn_out,
    preact,
    wide,
    send_rows,
    got_rows,
    send_slots,
    got_slots,
    back_rows,
    acts,
    cots,
    grads,
    firsts,
    seconds,
    outs,
    grads2,
    firsts2,
    seconds2,
    outs2,
    send_z,
    got_z,
    normed,
    query,
    keys,
    values,
    gates,
    attended,
    weights,
    slopes,
    total_a,
    total_b,
    residual,
    normed2,
    allowed_ref,
    root_ref,
    halo_send,
    halo_got,
    load_sem,
    send_sem,
    recv_sem,
    ready_sem,
    gather_send,
    gather_recv,
    pair_send,
    pair_recv,
    half_send,
    half_recv,
    z_send,
    z_recv,
    halo_sem,
):
    event, pack, tensor = where_am_i()
    me = event * 8 + pack
    core = lax.rem(event, 2)
    chip_x = event // 2
    partner = (event + 1 - 2 * core, pack, tensor)
    bf16, f32 = jnp.bfloat16, jnp.float32
    barrier = pltpu.get_barrier_semaphore()
    loads = []
    for number, (source, target) in enumerate(
        (
            (enc_hbm.at[0], enc.at[0]),
            (enc_hbm.at[1], enc.at[1]),
            (attn_in_hbm, attn_in.at[0]),
            (attn_out_hbm, attn_out.at[0]),
            (ffn_in_hbm, ffn_in.at[0]),
            (ffn_out_hbm, ffn_out.at[0]),
        )
    ):
        load = pltpu.make_async_copy(source, target, load_sem.at[number])
        load.start()
        loads.append(load)
    for step in range(1, 8):
        for device in (
            (event, lax.rem(pack + step, 8), tensor),
            (lax.rem(event + step, 8), pack, tensor),
        ):
            pl.semaphore_signal(barrier, inc=1, device_id=device, device_id_type=MESH)
    for step in (1, 3):
        pl.semaphore_signal(
            barrier,
            inc=1,
            device_id=(event, pack, lax.rem(tensor + step, 4)),
            device_id_type=MESH,
        )
    picks = routing(owner[...].astype(f32))
    slot_row = slot[...].astype(f32) + 1.0
    lane = lax.broadcasted_iota(jnp.int32, (GROUPS, 128), 1)
    slots = jnp.full((GROUPS, 128), -1.0, f32)
    for k in range(CAP):
        value = jnp.sum(jnp.where(picks[k], slot_row, 0.0), axis=1, keepdims=True) - 1.0
        slots = jnp.where(lane == k, value, slots)
    send_slots[:, 0, :] = slots
    pl.semaphore_wait(barrier, 16)
    for step in range(1, 8):
        pl.semaphore_signal(
            ready_sem,
            inc=1,
            device_id=(lax.rem(event + step, 8), pack, tensor),
            device_id_type=MESH,
        )

    gather = Gather(gather_send, gather_recv, event, pack, tensor)
    both = (pl.ds(0, 2), pl.ds(2, 2))

    def part_a(where, half=None):
        return attn_in.at[where, slice(None) if half is None else half, chip_x, core]

    def part_o(where, half=None):
        return attn_out.at[where, pack, core]

    def part_i(where, half=None):
        return ffn_in.at[where, slice(None) if half is None else half, core]

    def part_f(where, half=None):
        return ffn_out.at[where, pack, core, slice(None) if half is None else half]

    ring_f = TensorRing(gather, ffn_out_hbm.at[pack, core], part_f, (pl.ds(0, 1), pl.ds(1, 1)))
    ring_o = TensorRing(gather, attn_out_hbm.at[pack, core], part_o, (None, None))
    ring_a = TensorRing(gather, attn_in_hbm.at[:, chip_x, core], part_a, both)
    ring_i = TensorRing(gather, ffn_in_hbm.at[:, core], part_i, (pl.ds(0, 1), pl.ds(1, 1)))
    foreign = pl.ds(1, 3)

    def side_a(index, half=None):
        return attn_in.at[foreign, slice(None) if half is None else half, index, core]

    def side_o(index, half=None):
        return attn_out.at[foreign, index, core]

    def side_f(index, half=None):
        return ffn_out.at[foreign, index, core, slice(None) if half is None else half]

    x_a = SideRing(gather, 4, chip_x, gather.along_x, side_a, both)
    z_o = SideRing(gather, 8, pack, gather.along_z, side_o, (None, False))
    z_f = SideRing(gather, 8, pack, gather.along_z, side_f, (pl.ds(0, 1), pl.ds(1, 1)))

    ring_f.start()
    ring_o.start()
    loads[0].wait()
    acts[0, 0] = features[...]
    pre = dot32(features[...], enc[0])
    preact[...] = pre
    act = silu(pre).astype(bf16)
    acts[1, 0] = act
    ring_f.relay()
    ring_o.relay()
    ring_a.start()
    loads[1].wait()
    encoded = dot32(act, enc[1]).astype(bf16)
    ring_f.end()
    ring_o.end()
    z_f.start()
    z_o.start()
    for k in range(CAP):
        spread_rows(wide, k, dot32(one_hot(picks[k]), encoded))
    send_rows[...] = wide[...].astype(bf16).reshape(GROUPS, BLOCK_ROWS, 128)
    pl.semaphore_wait(ready_sem, 7)
    start_exchange(send_slots, got_slots, me, tensor, send_sem.at[0], recv_sem.at[0])
    start_exchange(send_rows, got_rows, me, tensor, send_sem.at[1], recv_sem.at[1])
    ring_a.relay()
    ring_i.start()
    ring_a.end()
    x_a.start()
    z_f.advance()
    z_o.advance()

    def pair_copy(number, array):
        return pltpu.make_async_remote_copy(
            src_ref=array.at[0],
            dst_ref=array.at[1],
            send_sem=pair_send.at[number],
            recv_sem=pair_recv.at[number],
            device_id=partner,
            device_id_type=MESH,
        )

    act_copies = [pair_copy(layer, acts.at[layer]) for layer in range(2)]
    for copy in act_copies:
        copy.start()
    end_exchange(send_slots, got_slots, send_sem.at[0], recv_sem.at[0])
    end_exchange(send_rows, got_rows, send_sem.at[1], recv_sem.at[1])
    wide[...] = got_rows[...].reshape(GROUPS * BLOCK_ROWS, 128).astype(f32)
    turned = jnp.concatenate([got_slots[:, 0, :], jnp.full((GROUPS, 128), -1.0, f32)], axis=0).T
    place = lax.broadcasted_iota(jnp.int32, (128, GROUPS), 0).astype(f32)
    total = None
    for k in range(CAP):
        pick = one_hot(turned[k : k + 1, :GROUPS] == place)
        term = dot32(pick, joined_rows(wide, k))
        total = term if total is None else total + term
    quarter = total
    normed_f, factor1 = norm_rows(quarter)
    halo_send[0] = normed_f.astype(bf16)
    normed[1] = normed_f.astype(bf16)
    residual[...] = quarter

    def halo_copy(number, target, shift):
        return pltpu.make_async_remote_copy(
            src_ref=halo_send.at[number],
            dst_ref=target,
            send_sem=halo_sem.at[number],
            recv_sem=halo_sem.at[2 + number],
            device_id=(event, pack, lax.rem(tensor + shift, 4)),
            device_id_type=MESH,
        )

    halo = halo_copy(0, normed.at[0], 1)
    halo.start()
    allowed, root = masks(documents, tensor)
    allowed_ref[...] = allowed
    root_ref[...] = jnp.broadcast_to(root, (128, 128))
    z_f.advance()
    z_o.advance()
    x_a.advance()
    z_f.advance()
    z_o.advance()
    ring_i.relay()
    z_f.advance()
    z_o.advance()
    x_a.advance()
    ring_i.end()
    gather.end()
    for load in loads[2:]:
        load.wait()
    halo.wait()
    own_rows = normed[1]
    all_rows = normed[...].reshape(256, 1024)
    total_a[...] = quarter

    def attend(slot_index, carry):
        def matrix(number):
            return attn_in[slot_index, number].reshape(1024, 256)

        query_f = rounded(dot32(own_rows, matrix(0)))
        gate = rounded(dot32(own_rows, matrix(3)))
        keys_f = rounded(dot32(all_rows, matrix(1)))
        values_f = rounded(dot32(all_rows, matrix(2)))
        gates[slot_index] = gate
        sides = []
        for ref, value in ((query, query_f), (keys, keys_f), (values, values_f)):
            pieces = by_parity(value)
            for parity in range(2):
                ref[slot_index, parity] = pieces[parity]
            sides.append(pieces)
        parts = []
        allowed = allowed_ref[...] > 0.5
        for pair in range(2):
            columns = slice(pair * 128, (pair + 1) * 128)
            part = None
            for parity in range(2):
                scores = (
                    dot32(sides[0][parity][:, columns], sides[1][parity][:, columns], ((1,), (1,)))
                    * HEAD_SCALE
                )
                sigma = jax.nn.sigmoid(scores)
                weight = jnp.where(allowed, scores * sigma, 0.0).astype(bf16)
                weights[slot_index, pair * 2 + parity] = weight
                slopes[slot_index, pair * 2 + parity] = jnp.where(
                    allowed, sigma * (1.0 + scores * (1.0 - sigma)), 0.0
                )
                term = dot32(weight, sides[2][parity][:, columns])
                part = term if part is None else part + term
            parts.append(part)
        result = jnp.concatenate(parts, axis=1) / root_ref[:, 0:1]
        attended[slot_index] = result
        gated = (result * silu(gate)).astype(bf16)
        total_a[...] += rounded(dot32(gated, attn_out[slot_index].reshape(256, 1024)))
        return carry

    lax.fori_loop(0, 4, attend, 0)
    resid = rounded(total_a[...])
    normed2_f, factor2 = norm_rows(resid)
    normed2[...] = normed2_f.astype(bf16)
    total_a[...] = resid
    total_b[...] = jnp.zeros((128, 1024), f32)

    def feed(slot_index, carry):
        rows = normed2[...]
        gate = dot32(rows, ffn_in[slot_index, 0].reshape(1024, 512))
        upper = dot32(rows, ffn_in[slot_index, 1].reshape(1024, 512))
        sigma = jax.nn.sigmoid(gate)
        active = gate * sigma
        down = ffn_out[slot_index].reshape(512, 1024)
        total_a[...] += rounded(dot32((active * upper).astype(bf16), down))
        d_hidden = dot32(out_grad[...], down, ((1,), (1,)))
        d_gate = (d_hidden * upper * (sigma * (1.0 + gate * (1.0 - sigma)))).astype(bf16)
        d_upper = (d_hidden * active).astype(bf16)
        total_b[...] += rounded(
            dot32(d_gate, ffn_in[slot_index, 0].reshape(1024, 512), ((1,), (1,)))
            + dot32(d_upper, ffn_in[slot_index, 1].reshape(1024, 512), ((1,), (1,)))
        )
        return carry

    lax.fori_loop(0, 4, feed, 0)
    packed_out[...] = total_a[...].astype(bf16)
    d_resid = (
        out_grad[...].astype(f32) + norm_back(total_b[...], normed2_f, factor2)
    ).astype(bf16)
    total_a[...] = jnp.zeros((128, 1024), f32)
    total_b[...] = jnp.zeros((128, 1024), f32)

    def attend_back(slot_index, carry):
        gate = gates[slot_index]
        d_gated = dot32(d_resid, attn_out[slot_index].reshape(256, 1024), ((1,), (1,)))
        sigma = jax.nn.sigmoid(gate)
        d_attended = by_parity(d_gated * (gate * sigma) / root_ref[:, 0:1])
        d_gate = (
            d_gated * attended[slot_index] * (sigma * (1.0 + gate * (1.0 - sigma)))
        ).astype(bf16)
        d_parts = [[], [], []]
        for pair in range(2):
            columns = slice(pair * 128, (pair + 1) * 128)
            sums = [None, None, None]
            for parity in range(2):
                head = pair * 2 + parity
                d_side = d_attended[parity][:, columns]
                d_weights = dot32(d_side, values[slot_index, parity, :, columns], ((1,), (1,)))
                d_scores = (d_weights * slopes[slot_index, head]).astype(bf16)
                terms = (
                    dot32(d_scores, keys[slot_index, parity, :, columns]),
                    dot32(d_scores, query[slot_index, parity, :, columns], ((0,), (0,))),
                    dot32(weights[slot_index, head], d_side, ((0,), (0,))),
                )
                for number, term in enumerate(terms):
                    sums[number] = term if sums[number] is None else sums[number] + term
            d_parts[0].append(sums[0] * HEAD_SCALE)
            d_parts[1].append(sums[1] * HEAD_SCALE)
            d_parts[2].append(sums[2])
        d_query, d_keys, d_values = (
            jnp.concatenate(parts, axis=1).astype(bf16) for parts in d_parts
        )
        keys_back = dot32(d_keys, attn_in[slot_index, 1].reshape(1024, 256), ((1,), (1,)))
        values_back = dot32(d_values, attn_in[slot_index, 2].reshape(1024, 256), ((1,), (1,)))
        both_back = keys_back + values_back
        total_b[...] += both_back[:128]
        total_a[...] += (
            both_back[128:]
            + dot32(d_query, attn_in[slot_index, 0].reshape(1024, 256), ((1,), (1,)))
            + dot32(d_gate, attn_in[slot_index, 3].reshape(1024, 256), ((1,), (1,)))
        )
        return carry

    lax.fori_loop(0, 4, attend_back, 0)
    halo_send[1] = total_b[...].astype(bf16)
    halo_back = halo_copy(1, halo_got, 3)
    halo_back.start()
    halo_back.wait()
    d_normed = total_a[...] + halo_got[...].astype(f32)
    normed_f, factor1 = norm_rows(residual[...])
    d_quarter = (d_resid.astype(f32) + norm_back(d_normed, normed_f, factor1)).astype(bf16)
    lane = lax.broadcasted_iota(jnp.int32, (GROUPS, 128), 1).astype(jnp.float32)
    for k in range(CAP):
        pick = one_hot(got_slots[:, 0, k : k + 1] == lane)
        spread_rows(wide, k, dot32(pick, d_quarter))
    send_rows[...] = wide[...].astype(jnp.bfloat16).reshape(GROUPS, BLOCK_ROWS, 128)
    start_exchange(send_rows, back_rows, me, tensor, send_sem.at[2], recv_sem.at[2])
    picks = routing(owner[...].astype(jnp.float32))
    for copy in act_copies:
        copy.wait()
    end_exchange(send_rows, back_rows, send_sem.at[2], recv_sem.at[2])
    wide[...] = back_rows[...].reshape(GROUPS * BLOCK_ROWS, 128).astype(jnp.float32)
    total = None
    for k in range(CAP):
        term = dot32(one_hot(picks[k]), joined_rows(wide, k), ((0,), (0,)))
        total = term if total is None else total + term
    cotangent = total.astype(jnp.bfloat16)
    row_grad[...] = cotangent
    cots[1, 0] = cotangent
    cot_copies = [pair_copy(2 + layer, cots.at[layer]) for layer in range(2)]
    cot_copies[1].start()
    pre = preact[...]
    sigma = jax.nn.sigmoid(pre)
    back = dot32(cotangent, enc[1], ((1,), (1,)))
    cots[0, 0] = (back * (sigma * (1.0 + pre * (1.0 - sigma)))).astype(jnp.bfloat16)
    cot_copies[0].start()

    def tensor_device(index):
        return (event, pack, index)

    def chip_device(index):
        return (index * 2 + core, pack, tensor)

    rings = ((chip_x, chip_device), (tensor, tensor_device))
    stages = [[], []]
    for layer in range(2):
        for stage, refs in enumerate(
            ((grads, firsts, seconds, outs), (grads2, firsts2, seconds2, outs2))
        ):
            index, device = rings[layer] if stage == 0 else rings[1 - layer]
            stages[stage].append(
                Halving(
                    *(ref.at[layer] for ref in refs),
                    (half_send, half_recv),
                    (stage * 2 + layer) * 6,
                    index,
                    device,
                )
            )
    for layer in (1, 0):
        cot_copies[layer].wait()
        cot = cots[layer].reshape(256, 1024)
        for chip in range(4):
            columns = pl.ds(pl.multiple_of((chip * 2 + core) * 128, 128), 128)
            act = acts[layer, :, :, columns].reshape(256, 128)
            term = dot32(act, cot, ((0,), (0,))).astype(jnp.bfloat16)
            for block in range(4):
                for half in range(2):
                    piece = term[half * 64 : (half + 1) * 64, block * 256 : (block + 1) * 256]
                    if layer == 1:
                        grads[layer, block, half, chip] = piece
                    else:
                        grads[layer, chip, half, block] = piece
        stages[0][layer].start_one()
    for layer in (1, 0):
        stages[0][layer].start_two()
    for layer in (1, 0):
        for half, value in enumerate(stages[0][layer].finish()):
            for block in range(4):
                grads2[layer, block, half] = value[block]
        stages[1][layer].start_one()
    for layer in (1, 0):
        stages[1][layer].start_two()
    for layer in (1, 0):
        for half, value in enumerate(stages[1][layer].finish()):
            for quarter in range(4):
                send_z[half * 4 + quarter, layer] = value[quarter * 16 : (quarter + 1) * 16]
    z_copies = []
    for step in (1, 7, 2, 6, 3, 5, 4):
        other = lax.rem(pack + step, 8)
        z_copies.append(
            pltpu.make_async_remote_copy(
                src_ref=send_z.at[other],
                dst_ref=got_z.at[pack],
                send_sem=z_send.at[step],
                recv_sem=z_recv.at[step],
                device_id=(event, other, tensor),
                device_id_type=MESH,
            )
        )
        z_copies[-1].start()
    got_z[pack] = send_z[pack]
    for copy in z_copies:
        copy.wait()
    total = got_z[0].astype(jnp.float32)
    for source in range(1, 8):
        total = total + got_z[source].astype(jnp.float32)
    enc_grad[...] = total


def shards(
    features,
    dest_owner,
    dest_slot,
    doc_ids,
    enc_weight,
    attn_in,
    attn_out,
    ffn_in,
    ffn_out,
    out_grad,
):
    bf16, f32 = jnp.bfloat16, jnp.float32
    vmem = pl.BlockSpec(memory_space=pltpu.VMEM)
    hbm = pl.BlockSpec(memory_space=pl.ANY)
    dma = pltpu.SemaphoreType.DMA
    packed_out, row_grad, enc_grad = pl.pallas_call(
        step_kernel,
        out_shape=(
            jax.ShapeDtypeStruct((128, 1024), bf16),
            jax.ShapeDtypeStruct((128, 1024), bf16),
            jax.ShapeDtypeStruct((2, 16, 256), f32),
        ),
        in_specs=[vmem] * 5 + [hbm] * 5,
        out_specs=(vmem, vmem, vmem),
        scratch_shapes=[
            pltpu.VMEM((2, 1024, 1024), bf16),
            pltpu.VMEM((4, 4, 4, 2, 128, 256), bf16),
            pltpu.VMEM((4, 8, 2, 16, 1024), bf16),
            pltpu.VMEM((4, 2, 2, 512, 512), bf16),
            pltpu.VMEM((4, 8, 2, 2, 16, 1024), bf16),
            pltpu.VMEM((128, 1024), f32),
            pltpu.VMEM((GROUPS * BLOCK_ROWS, 128), f32),
            pltpu.VMEM((GROUPS, BLOCK_ROWS, 128), bf16),
            pltpu.VMEM((GROUPS, BLOCK_ROWS, 128), bf16),
            pltpu.VMEM((GROUPS, 1, 128), f32),
            pltpu.VMEM((GROUPS, 1, 128), f32),
            pltpu.VMEM((GROUPS, BLOCK_ROWS, 128), bf16),
            pltpu.VMEM((2, 2, 128, 1024), bf16),
            pltpu.VMEM((2, 2, 128, 1024), bf16),
            pltpu.VMEM((2, 4, 2, 4, 64, 256), bf16),
            pltpu.VMEM((2, 2, 2, 4, 64, 256), bf16),
            pltpu.VMEM((2, 2, 4, 64, 256), bf16),
            pltpu.VMEM((2, 2, 4, 64, 256), bf16),
            pltpu.VMEM((2, 4, 2, 64, 256), bf16),
            pltpu.VMEM((2, 2, 2, 64, 256), bf16),
            pltpu.VMEM((2, 2, 64, 256), bf16),
            pltpu.VMEM((2, 2, 64, 256), bf16),
            pltpu.VMEM((8, 2, 16, 256), bf16),
            pltpu.VMEM((8, 2, 16, 256), bf16),
            pltpu.VMEM((2, 128, 1024), bf16),
            pltpu.VMEM((4, 2, 128, 256), bf16),
            pltpu.VMEM((4, 2, 256, 256), bf16),
            pltpu.VMEM((4, 2, 256, 256), bf16),
            pltpu.VMEM((4, 128, 256), f32),
            pltpu.VMEM((4, 128, 256), f32),
            pltpu.VMEM((4, 4, 128, 256), bf16),
            pltpu.VMEM((4, 4, 128, 256), f32),
            pltpu.VMEM((128, 1024), f32),
            pltpu.VMEM((128, 1024), f32),
            pltpu.VMEM((128, 1024), f32),
            pltpu.VMEM((128, 1024), bf16),
            pltpu.VMEM((128, 256), f32),
            pltpu.VMEM((128, 128), f32),
            pltpu.VMEM((2, 128, 1024), bf16),
            pltpu.VMEM((128, 1024), bf16),
            dma((6,)),
            dma((3,)),
            dma((3,)),
            pltpu.SemaphoreType.REGULAR,
            dma((64,)),
            dma((64,)),
            dma((4,)),
            dma((4,)),
            dma((24,)),
            dma((24,)),
            dma((8,)),
            dma((8,)),
            dma((4,)),
        ],
        compiler_params=pltpu.CompilerParams(
            collective_id=0, has_side_effects=True, vmem_limit_bytes=VMEM_LIMIT
        ),
        name="train_step",
    )(
        features,
        dest_owner.reshape(1, 128),
        dest_slot.reshape(1, 128),
        doc_ids,
        out_grad[0],
        enc_weight,
        attn_in.reshape(4, 4, 2, 128, 256),
        attn_out.reshape(8, 2, 16, 1024),
        ffn_in.reshape(2, 2, 512, 512),
        ffn_out.reshape(8, 2, 2, 16, 1024),
    )
    return (packed_out[None], row_grad, enc_grad)


def solution(mesh):
    placed = (
        P(("event", "pack", "tensor"), None),
        P(("event", "pack", "tensor")),
        P(("event", "pack", "tensor")),
        P(("event", "pack"), None),
        P(),
        P(None, None, "tensor"),
        P("tensor", None),
        P(None, None, "tensor"),
        P("tensor", None),
        P(("event", "pack"), "tensor", None),
    )
    return jax.shard_map(
        shards,
        mesh=mesh,
        in_specs=placed,
        out_specs=(
            P(("event", "pack"), "tensor", None),
            P(("event", "pack", "tensor"), None),
            P(None, ("event", "pack"), "tensor"),
        ),
        check_vma=False,
    )
```

```python
import jax
import jax.numpy as jnp
from jax import lax
from jax.experimental import pallas as pl
from jax.experimental.pallas import tpu as pltpu
from jax.sharding import PartitionSpec as P

MESH = pl.DeviceIdType.MESH
EPS = 1e-06
GROUPS = 64
CAP = 3
BLOCK_ROWS = CAP * 8
VMEM_LIMIT = 63 * 1024 * 1024
HEAD_SCALE = 64**-0.5


def silu_grad(value):
    sigma = jax.nn.sigmoid(value)
    return sigma * (1.0 + value * (1.0 - sigma))


def norm_rows(rows):
    factor = lax.rsqrt(jnp.mean(rows * rows, axis=-1, keepdims=True) + EPS)
    return (rows * factor, factor)


def norm_back(grad, normed, factor):
    return factor * (grad - normed * jnp.mean(grad * normed, axis=-1, keepdims=True))


def where_am_i():
    return (lax.axis_index("event"), lax.axis_index("pack"), lax.axis_index("tensor"))


def peer(index, tensor):
    return (index // 8, lax.rem(index, 8), tensor)


def greet_all(barrier, me, tensor):
    def greet(step, carry):
        pl.semaphore_signal(
            barrier, inc=1, device_id=peer(lax.rem(me + step, GROUPS), tensor), device_id_type=MESH
        )
        return carry

    lax.fori_loop(1, GROUPS, greet, 0)


def exchange_copy(source, target, me, tensor, step, send_sem, recv_sem):
    other = lax.rem(me + step, GROUPS)
    return pltpu.make_async_remote_copy(
        src_ref=source.at[other],
        dst_ref=target.at[me],
        send_sem=send_sem,
        recv_sem=recv_sem,
        device_id=peer(other, tensor),
        device_id_type=MESH,
    )


def start_exchange(source, target, me, tensor, send_sem, recv_sem):
    def start(step, carry):
        exchange_copy(source, target, me, tensor, step, send_sem, recv_sem).start()
        return carry

    lax.fori_loop(1, GROUPS, start, 0)
    target[me] = source[me]


def await_bytes(ref, sem):
    pltpu.make_async_copy(ref, ref, sem).wait()


def end_exchange(source, target, send_sem, recv_sem):
    await_bytes(source.at[pl.ds(0, GROUPS - 1)], send_sem)
    await_bytes(target.at[pl.ds(0, GROUPS - 1)], recv_sem)


def dot32(left, right, dims=((1,), (0,))):
    return lax.dot_general(left, right, (dims, ((), ())), preferred_element_type=jnp.float32)


def routing(owner_row):
    rows = jnp.broadcast_to(owner_row, (128, 128))
    columns = rows.T
    earlier = lax.broadcasted_iota(jnp.int32, (128, 128), 0) < lax.broadcasted_iota(
        jnp.int32, (128, 128), 1
    )
    rank = jnp.sum(jnp.where((columns == rows) & earlier, 1.0, 0.0), axis=0, keepdims=True)
    group = lax.broadcasted_iota(jnp.int32, (GROUPS, 128), 0).astype(jnp.float32)
    mine = owner_row == group
    return [mine & (rank == float(k)) for k in range(CAP)]


def one_hot(mask):
    return jnp.where(mask, 1.0, 0.0).astype(jnp.bfloat16)


def spread_rows(wide, k, rows):
    for part in range(8):
        wide[pl.ds(k * 8 + part, GROUPS, stride=BLOCK_ROWS), :] = rows[
            :, part * 128 : (part + 1) * 128
        ]


def joined_rows(wide, k):
    return jnp.concatenate(
        [wide[pl.ds(k * 8 + part, GROUPS, stride=BLOCK_ROWS), :] for part in range(8)], axis=1
    ).astype(jnp.bfloat16)


def silu(value):
    return value * jax.nn.sigmoid(value)


class Halving:
    def __init__(self, blocks, first, second, outgoing, sems, base, index, device):
        self.blocks, self.first, self.second, self.outgoing = blocks, first, second, outgoing
        self.sems, self.base, self.index = sems, base, index
        near = index + 1 - 2 * lax.rem(index, 2)
        self.other = (near, 3 - index)
        self.far = lax.rem(index + 2, 4)
        self.device = device

    def copy(self, source, target, number, half_partner):
        send, recv = self.sems
        return pltpu.make_async_remote_copy(
            src_ref=source,
            dst_ref=target,
            send_sem=send.at[self.base + number],
            recv_sem=recv.at[self.base + number],
            device_id=self.device(half_partner),
            device_id_type=MESH,
        )

    def round_one(self):
        copies = []
        for half in range(2):
            partner = self.other[half]
            for slot, block in enumerate((partner, self.far)):
                copies.append(
                    self.copy(
                        self.blocks.at[block, half],
                        self.first.at[half, slot],
                        half * 2 + slot,
                        partner,
                    )
                )
        return copies

    def round_two(self):
        return [
            self.copy(self.outgoing.at[half], self.second.at[half], 4 + half, self.other[1 - half])
            for half in range(2)
        ]

    def start_one(self):
        for copy in self.round_one():
            copy.start()

    def start_two(self):
        for copy in self.round_one():
            copy.wait()
        for half in range(2):
            block = self.other[1 - half]
            self.outgoing[half] = (
                self.blocks[block, half].astype(jnp.float32)
                + self.first[half, 1].astype(jnp.float32)
            ).astype(jnp.bfloat16)
        for copy in self.round_two():
            copy.start()

    def finish(self):
        for copy in self.round_two():
            copy.wait()
        return [
            (
                self.blocks[self.index, half].astype(jnp.float32)
                + self.first[half, 0].astype(jnp.float32)
                + self.second[half].astype(jnp.float32)
            ).astype(jnp.bfloat16)
            for half in range(2)
        ]


class Gather:
    def __init__(self, send, recv, event, pack, tensor):
        self.send, self.recv = send, recv
        self.event, self.pack, self.tensor = event, pack, tensor
        self.core = lax.rem(event, 2)
        self.used = 0
        self.started = []
        self.partner = (event + 1 - 2 * self.core, pack, tensor)
        self.pair_started = []

    def copy(self, source, target, device):
        number = self.used
        self.used += 1
        copy = pltpu.make_async_remote_copy(
            src_ref=source,
            dst_ref=target,
            send_sem=self.send.at[number],
            recv_sem=self.recv.at[number],
            device_id=device,
            device_id_type=MESH,
        )
        copy.start()
        self.started.append(copy)
        return copy

    def along_tensor(self, shift):
        return (self.event, self.pack, lax.rem(self.tensor + shift + 4, 4))

    def along_x(self, shift):
        return (lax.rem(self.event + 2 * shift + 8, 8), self.pack, self.tensor)

    def along_z(self, shift):
        return (self.event, lax.rem(self.pack + shift + 8, 8), self.tensor)

    def to_pair(self, region, name):
        self.pair_started.append((name, self.copy(region, region, self.partner)))

    def await_pair(self, names):
        for name, copy in self.pair_started:
            if name in names:
                copy.wait_recv()

    def end(self):
        for copy in self.started:
            copy.wait_send()


class TensorRing:
    def __init__(self, gather, name, own, region, halves):
        self.gather, self.name, self.own = gather, name, own
        self.region, self.halves = region, halves

    def start(self):
        device = self.gather.along_tensor
        self.near = [
            self.gather.copy(self.own, self.region(2), device(1)),
            self.gather.copy(self.own, self.region(1), device(-1)),
        ]

    def relay(self):
        for copy in self.near:
            copy.wait_recv()
        device = self.gather.along_tensor
        plus, minus = self.halves
        self.far = []
        if plus is not False:
            self.far.append(self.gather.copy(self.region(2, plus), self.region(3, plus), device(1)))
        if minus is not False:
            self.far.append(
                self.gather.copy(self.region(1, minus), self.region(3, minus), device(-1))
            )

    def end(self):
        for copy in self.far:
            copy.wait_recv()
        self.gather.to_pair(self.region(pl.ds(1, 3)), self.name)


class SideRing:
    def __init__(self, gather, name, size, index, device, region, halves):
        self.gather, self.name, self.size, self.index = gather, name, size, index
        self.device, self.region, self.halves = device, region, halves
        self.step = 0
        self.flying = None

    def block(self, shift, half=None):
        return self.region(lax.rem(self.index + shift + self.size, self.size), half)

    def start(self):
        block = self.block(0)
        self.flying = [
            self.gather.copy(block, block, self.device(1)),
            self.gather.copy(block, block, self.device(-1)),
        ]
        self.step = 1

    def advance(self):
        for copy in self.flying:
            copy.wait_recv()
        step = self.step
        last = step == self.size // 2
        forward = []
        if not last:
            halves = (None, None) if step + 1 < self.size // 2 else self.halves
            for sign, half in zip((1, -1), halves):
                if half is not False:
                    block = self.block(-sign * step, half)
                    forward.append(self.gather.copy(block, block, self.device(sign)))
            for sign in (1, -1):
                self.gather.to_pair(self.block(-sign * step), self.name)
        else:
            self.gather.to_pair(self.block(step), self.name)
        self.flying = forward
        self.step = step + 1


def masks(documents, tensor):
    own = documents[:, pl.ds(pl.multiple_of(tensor * 128, 128), 128)].astype(jnp.float32)
    before = documents[
        :, pl.ds(pl.multiple_of(lax.rem(tensor + 3, 4) * 128, 128), 128)
    ].astype(jnp.float32)
    before = before - jnp.where(tensor == 0, 1000.0, 0.0)
    mine = jnp.broadcast_to(own, (128, 128)).T
    row = lax.broadcasted_iota(jnp.int32, (128, 128), 0)
    column = lax.broadcasted_iota(jnp.int32, (128, 128), 1)
    allowed = jnp.concatenate(
        [
            jnp.where(mine == before, 1.0, 0.0),
            jnp.where((mine == own) & (column <= row), 1.0, 0.0),
        ],
        axis=1,
    )
    root = jnp.sqrt(jnp.sum(allowed, axis=1, keepdims=True))
    return (allowed, root)


def by_parity(value):
    first = lax.rem(lax.broadcasted_iota(jnp.int32, value.shape, 1), 128) < 64
    return (
        jnp.where(first, value, 0.0).astype(jnp.bfloat16),
        jnp.where(first, 0.0, value).astype(jnp.bfloat16),
    )


def rounded(value):
    return value.astype(jnp.bfloat16).astype(jnp.float32)


def step_kernel(
    features,
    owner,
    slot,
    documents,
    out_grad,
    enc_hbm,
    first_hbm,
    second_hbm,
    attn_out_hbm,
    gate_hbm,
    up_hbm,
    down_z_hbm,
    down_t_hbm,
    packed_out,
    row_grad,
    enc_grad,
    enc,
    first,
    second,
    attn_out,
    gate_in,
    up_in,
    down_z,
    down_t,
    preact,
    wide,
    send_rows,
    got_rows,
    send_slots,
    got_slots,
    back_rows,
    acts,
    cots,
    grads,
    firsts,
    seconds,
    outs,
    grads2,
    firsts2,
    seconds2,
    outs2,
    send_z,
    got_z,
    normed,
    query,
    keys,
    values,
    gates,
    attended,
    weights,
    slopes,
    total_a,
    total_b,
    residual,
    normed2,
    allowed_ref,
    root_ref,
    d_proj,
    gated,
    halo_send,
    halo_got,
    load_sem,
    send_sem,
    recv_sem,
    ready_sem,
    gather_send,
    gather_recv,
    pair_send,
    pair_recv,
    half_send,
    half_recv,
    z_send,
    z_recv,
    halo_sem,
):
    event, pack, tensor = where_am_i()
    me = event * 8 + pack
    core = lax.rem(event, 2)
    chip_x = event // 2
    partner = (event + 1 - 2 * core, pack, tensor)
    bf16, f32 = jnp.bfloat16, jnp.float32
    barrier = pltpu.get_barrier_semaphore()
    loads = []
    for number, (source, target) in enumerate(
        (
            (enc_hbm.at[0], enc.at[0]),
            (enc_hbm.at[1], enc.at[1]),
            (first_hbm.at[pl.ds(0, 2)], first.at[0]),
            (second_hbm.at[pl.ds(2, 2)], second.at[0]),
            (attn_out_hbm, attn_out.at[0]),
            (gate_hbm.at[0], gate_in.at[0]),
            (up_hbm.at[1], up_in.at[0]),
            (down_z_hbm.at[0], down_z.at[0]),
            (down_t_hbm.at[1], down_t.at[0]),
        )
    ):
        load = pltpu.make_async_copy(source, target, load_sem.at[number])
        load.start()
        loads.append(load)
    for step in range(1, 8):
        for device in (
            (event, lax.rem(pack + step, 8), tensor),
            (lax.rem(event + step, 8), pack, tensor),
        ):
            pl.semaphore_signal(barrier, inc=1, device_id=device, device_id_type=MESH)
    for step in (1, 3):
        pl.semaphore_signal(
            barrier,
            inc=1,
            device_id=(event, pack, lax.rem(tensor + step, 4)),
            device_id_type=MESH,
        )
    picks = routing(owner[...].astype(f32))
    slot_row = slot[...].astype(f32) + 1.0
    lane = lax.broadcasted_iota(jnp.int32, (GROUPS, 128), 1)
    slots = jnp.full((GROUPS, 128), -1.0, f32)
    for k in range(CAP):
        value = jnp.sum(jnp.where(picks[k], slot_row, 0.0), axis=1, keepdims=True) - 1.0
        slots = jnp.where(lane == k, value, slots)
    send_slots[:, 0, :] = slots
    for k in range(CAP):
        spread_rows(wide, k, dot32(one_hot(picks[k]), features[...]))
    send_rows[...] = wide[...].astype(bf16).reshape(GROUPS, BLOCK_ROWS, 128)
    pl.semaphore_wait(barrier, 16)
    for step in range(1, 8):
        pl.semaphore_signal(
            ready_sem,
            inc=1,
            device_id=(lax.rem(event + step, 8), pack, tensor),
            device_id_type=MESH,
        )

    gather = Gather(gather_send, gather_recv, event, pack, tensor)
    whole = slice(None)
    low, high = pl.ds(0, 1), pl.ds(1, 1)
    foreign = pl.ds(1, 3)

    def part_of(half):
        return whole if half is None else half

    def first_at(where, index, half=None):
        return first.at[where, part_of(half), index, core]

    def second_at(where, index, half=None):
        return second.at[where, part_of(half), index, core]

    def attn_out_at(where, index, half=None):
        return attn_out.at[where, index, core, part_of(half)]

    def gate_at(where, index, half=None):
        return gate_in.at[where, index, core, part_of(half)]

    def down_z_at(where, index, half=None):
        return down_z.at[where, index, core]

    def up_at(where, half=None):
        return up_in.at[where, core, part_of(half)]

    def down_t_at(where, half=None):
        return down_t.at[where, core, part_of(half)]

    def slice_ring(name, own, region, index, halves):
        return TensorRing(
            gather, name, own, lambda where, half=None: region(where, index, half), halves
        )

    t_first = slice_ring(
        "attn", first_hbm.at[pl.ds(0, 2), chip_x, core], first_at, chip_x, (low, high)
    )
    t_second = slice_ring(
        "attn", second_hbm.at[pl.ds(2, 2), pack, core], second_at, pack, (low, high)
    )
    t_out = slice_ring("out", attn_out_hbm.at[chip_x, core], attn_out_at, chip_x, (low, high))
    t_gate = slice_ring("ffn", gate_hbm.at[0, chip_x, core], gate_at, chip_x, (low, high))
    t_down = slice_ring("ffn", down_z_hbm.at[0, pack, core], down_z_at, pack, (False, None))
    t_up = TensorRing(gather, "ffn", up_hbm.at[1, core], up_at, (low, high))
    t_last = TensorRing(gather, "ffn", down_t_hbm.at[1, core], down_t_at, (low, high))

    def side_ring(name, axis, region, halves):
        size, index, device = (
            (4, chip_x, gather.along_x) if axis == "x" else (8, pack, gather.along_z)
        )
        return SideRing(
            gather,
            name,
            size,
            index,
            device,
            lambda number, half=None: region(foreign, number, half),
            halves,
        )

    x_first = side_ring("attn", "x", first_at, (low, high))
    z_second = side_ring("attn", "z", second_at, (low, high))
    x_out = side_ring("out", "x", attn_out_at, (low, high))
    x_gate = side_ring("ffn", "x", gate_at, (low, high))
    z_down = side_ring("ffn", "z", down_z_at, (None, False))

    t_second.start()
    t_first.start()
    t_down.start()
    t_out.start()
    t_gate.start()
    pl.semaphore_wait(ready_sem, 7)
    start_exchange(send_slots, got_slots, me, tensor, send_sem.at[0], recv_sem.at[0])
    start_exchange(send_rows, got_rows, me, tensor, send_sem.at[1], recv_sem.at[1])
    t_second.relay()
    t_first.relay()
    t_down.relay()
    t_out.relay()
    t_gate.relay()
    t_up.start()
    t_second.end()
    z_second.start()
    t_first.end()
    x_first.start()
    t_down.end()
    z_down.start()
    t_out.end()
    x_out.start()
    t_gate.end()
    allowed, root = masks(documents, tensor)
    allowed_ref[...] = allowed
    root_ref[...] = jnp.broadcast_to(root, (128, 128))

    def pair_copy(number, array):
        return pltpu.make_async_remote_copy(
            src_ref=array.at[0],
            dst_ref=array.at[1],
            send_sem=pair_send.at[number],
            recv_sem=pair_recv.at[number],
            device_id=partner,
            device_id_type=MESH,
        )

    end_exchange(send_slots, got_slots, send_sem.at[0], recv_sem.at[0])
    end_exchange(send_rows, got_rows, send_sem.at[1], recv_sem.at[1])
    wide[...] = got_rows[...].reshape(GROUPS * BLOCK_ROWS, 128).astype(f32)
    turned = jnp.concatenate([got_slots[:, 0, :], jnp.full((GROUPS, 128), -1.0, f32)], axis=0).T
    place = lax.broadcasted_iota(jnp.int32, (128, GROUPS), 0).astype(f32)
    total = None
    for k in range(CAP):
        pick = one_hot(turned[k : k + 1, :GROUPS] == place)
        term = dot32(pick, joined_rows(wide, k))
        total = term if total is None else total + term
    rows = total.astype(bf16)
    for load in loads[:2]:
        load.wait()
    pre = dot32(rows, enc[0])
    preact[...] = pre
    act = silu(pre).astype(bf16)
    quarter = rounded(dot32(act, enc[1]))
    normed_f, factor1 = norm_rows(quarter)
    halo_send[0] = normed_f.astype(bf16)
    normed[1] = normed_f.astype(bf16)
    residual[...] = quarter

    def halo_copy(number, target, shift):
        return pltpu.make_async_remote_copy(
            src_ref=halo_send.at[number],
            dst_ref=target,
            send_sem=halo_sem.at[number],
            recv_sem=halo_sem.at[2 + number],
            device_id=(event, pack, lax.rem(tensor + shift, 4)),
            device_id_type=MESH,
        )

    halo = halo_copy(0, normed.at[0], 1)
    halo.start()
    acts[0, 0] = rows
    acts[1, 0] = act
    act_copies = [pair_copy(layer, acts.at[layer]) for layer in range(2)]
    for copy in act_copies:
        copy.start()
    t_last.start()
    z_second.advance()
    x_first.advance()
    x_gate.start()
    z_down.advance()
    x_out.advance()
    z_second.advance()
    t_up.relay()
    z_down.advance()
    x_first.advance()
    z_second.advance()
    z_down.advance()
    z_second.advance()
    t_last.relay()
    x_gate.advance()
    gather.await_pair(("attn",))
    for load in loads[2:4]:
        load.wait()
    halo.wait()
    own_rows = normed[1]
    all_rows = normed[...].reshape(256, 1024)
    total_a[...] = quarter

    def matrix(slot_index, number):
        source = first if number < 2 else second
        return source[slot_index, number % 2].reshape(1024, 256)

    def attend(slot_index):
        query_f = rounded(dot32(own_rows, matrix(slot_index, 0)))
        gate = rounded(dot32(own_rows, matrix(slot_index, 3)))
        keys_f = rounded(dot32(all_rows, matrix(slot_index, 1)))
        values_f = rounded(dot32(all_rows, matrix(slot_index, 2)))
        gates[slot_index] = gate
        sides = []
        for ref, value in ((query, query_f), (keys, keys_f), (values, values_f)):
            pieces = by_parity(value)
            for parity in range(2):
                ref[slot_index, parity] = pieces[parity]
            sides.append(pieces)
        parts = []
        allowed = allowed_ref[...] > 0.5
        for pair in range(2):
            columns = slice(pair * 128, (pair + 1) * 128)
            part = None
            for parity in range(2):
                scores = (
                    dot32(sides[0][parity][:, columns], sides[1][parity][:, columns], ((1,), (1,)))
                    * HEAD_SCALE
                )
                sigma = jax.nn.sigmoid(scores)
                weight = jnp.where(allowed, scores * sigma, 0.0).astype(bf16)
                weights[slot_index, pair * 2 + parity] = weight
                slopes[slot_index, pair * 2 + parity] = jnp.where(
                    allowed, sigma * (1.0 + scores * (1.0 - sigma)), 0.0
                )
                term = dot32(weight, sides[2][parity][:, columns])
                part = term if part is None else part + term
            parts.append(part)
        result = jnp.concatenate(parts, axis=1) / root_ref[:, 0:1]
        attended[slot_index] = result
        gated[slot_index] = (result * silu(gate)).astype(bf16)

    attend(0)
    z_down.advance()
    attend(1)
    attend(2)
    x_out.advance()
    attend(3)
    gather.await_pair(("out",))
    loads[4].wait()
    for slot_index in range(4):
        total_a[...] += rounded(
            dot32(gated[slot_index], attn_out[slot_index].reshape(256, 1024))
        )
    resid = rounded(total_a[...])
    normed2_f, factor2 = norm_rows(resid)
    normed2[...] = normed2_f.astype(bf16)
    total_a[...] = resid
    total_b[...] = jnp.zeros((128, 1024), f32)

    def feed(slot_index, carry):
        rows = normed2[...]
        gate = dot32(rows, gate_in[slot_index].reshape(1024, 512))
        upper = dot32(rows, up_in[slot_index].reshape(1024, 512))
        sigma = jax.nn.sigmoid(gate)
        active = gate * sigma
        down = (down_z[slot_index].reshape(256, 1024), down_t[slot_index].reshape(256, 1024))
        hidden = (active * upper).astype(bf16)
        total_a[...] += rounded(dot32(hidden[:, :256], down[0]) + dot32(hidden[:, 256:], down[1]))
        d_hidden = jnp.concatenate(
            [dot32(out_grad[...], part, ((1,), (1,))) for part in down], axis=1
        )
        d_gate = (d_hidden * upper * (sigma * (1.0 + gate * (1.0 - sigma)))).astype(bf16)
        d_upper = (d_hidden * active).astype(bf16)
        total_b[...] += rounded(
            dot32(d_gate, gate_in[slot_index].reshape(1024, 512), ((1,), (1,)))
            + dot32(d_upper, up_in[slot_index].reshape(1024, 512), ((1,), (1,)))
        )
        return carry

    x_gate.advance()
    t_up.end()
    t_last.end()
    gather.await_pair(("ffn",))
    for load in loads[5:]:
        load.wait()
    lax.fori_loop(0, 4, feed, 0)
    packed_out[...] = total_a[...].astype(bf16)
    d_resid = (
        out_grad[...].astype(f32) + norm_back(total_b[...], normed2_f, factor2)
    ).astype(bf16)
    total_a[...] = jnp.zeros((128, 1024), f32)
    total_b[...] = jnp.zeros((128, 1024), f32)

    def attend_back(slot_index, carry):
        gate = gates[slot_index]
        d_gated = dot32(d_resid, attn_out[slot_index].reshape(256, 1024), ((1,), (1,)))
        sigma = jax.nn.sigmoid(gate)
        d_attended = by_parity(d_gated * (gate * sigma) / root_ref[:, 0:1])
        d_gate = (
            d_gated * attended[slot_index] * (sigma * (1.0 + gate * (1.0 - sigma)))
        ).astype(bf16)
        d_parts = [[], [], []]
        for pair in range(2):
            columns = slice(pair * 128, (pair + 1) * 128)
            sums = [None, None, None]
            for parity in range(2):
                head = pair * 2 + parity
                d_side = d_attended[parity][:, columns]
                d_weights = dot32(d_side, values[slot_index, parity, :, columns], ((1,), (1,)))
                d_scores = (d_weights * slopes[slot_index, head]).astype(bf16)
                terms = (
                    dot32(d_scores, keys[slot_index, parity, :, columns]),
                    dot32(d_scores, query[slot_index, parity, :, columns], ((0,), (0,))),
                    dot32(weights[slot_index, head], d_side, ((0,), (0,))),
                )
                for number, term in enumerate(terms):
                    sums[number] = term if sums[number] is None else sums[number] + term
            d_parts[0].append(sums[0] * HEAD_SCALE)
            d_parts[1].append(sums[1] * HEAD_SCALE)
            d_parts[2].append(sums[2])
        d_query, d_keys, d_values = (
            jnp.concatenate(parts, axis=1).astype(bf16) for parts in d_parts
        )
        for number, value in enumerate((d_query, d_keys[128:], d_values[128:], d_gate)):
            d_proj[slot_index, number] = value
        total_b[...] += dot32(d_keys[:128], matrix(slot_index, 1), ((1,), (1,))) + dot32(
            d_values[:128], matrix(slot_index, 2), ((1,), (1,))
        )
        return carry

    lax.fori_loop(0, 4, attend_back, 0)
    halo_send[1] = total_b[...].astype(bf16)
    halo_back = halo_copy(1, halo_got, 3)
    halo_back.start()

    def project_back(slot_index, carry):
        total_a[...] += sum(
            dot32(d_proj[slot_index, number], matrix(slot_index, number), ((1,), (1,)))
            for number in range(4)
        )
        return carry

    lax.fori_loop(0, 4, project_back, 0)
    halo_back.wait()
    d_normed = total_a[...] + halo_got[...].astype(f32)
    normed_f, factor1 = norm_rows(residual[...])
    d_quarter = (d_resid.astype(f32) + norm_back(d_normed, normed_f, factor1)).astype(bf16)
    cots[1, 0] = d_quarter
    cot_copies = [pair_copy(2 + layer, cots.at[layer]) for layer in range(2)]
    cot_copies[1].start()
    lane = lax.broadcasted_iota(jnp.int32, (GROUPS, 128), 1).astype(jnp.float32)
    for k in range(CAP):
        chosen = one_hot(got_slots[:, 0, k : k + 1] == lane)
        spread_rows(wide, k, dot32(chosen, d_quarter))
    send_rows[...] = wide[...].astype(bf16).reshape(GROUPS, BLOCK_ROWS, 128)
    start_exchange(send_rows, back_rows, me, tensor, send_sem.at[2], recv_sem.at[2])
    cots[0, 0] = (
        dot32(d_quarter, enc[1], ((1,), (1,))) * silu_grad(preact[...])
    ).astype(bf16)
    cot_copies[0].start()
    for copy in act_copies:
        copy.wait()

    def tensor_device(index):
        return (event, pack, index)

    def chip_device(index):
        return (index * 2 + core, pack, tensor)

    rings = ((chip_x, chip_device), (tensor, tensor_device))
    stages = [[], []]
    for layer in range(2):
        for stage, refs in enumerate(
            ((grads, firsts, seconds, outs), (grads2, firsts2, seconds2, outs2))
        ):
            index, device = rings[layer] if stage == 0 else rings[1 - layer]
            stages[stage].append(
                Halving(
                    *(ref.at[layer] for ref in refs),
                    (half_send, half_recv),
                    (stage * 2 + layer) * 6,
                    index,
                    device,
                )
            )
    for layer in (1, 0):
        cot_copies[layer].wait()
        cot = cots[layer].reshape(256, 1024)
        for chip in range(4):
            columns = pl.ds(pl.multiple_of((chip * 2 + core) * 128, 128), 128)
            act = acts[layer, :, :, columns].reshape(256, 128)
            term = dot32(act, cot, ((0,), (0,))).astype(jnp.bfloat16)
            for block in range(4):
                for half in range(2):
                    piece = term[half * 64 : (half + 1) * 64, block * 256 : (block + 1) * 256]
                    if layer == 1:
                        grads[layer, block, half, chip] = piece
                    else:
                        grads[layer, chip, half, block] = piece
        stages[0][layer].start_one()
    for layer in (1, 0):
        stages[0][layer].start_two()
    for layer in (1, 0):
        for half, value in enumerate(stages[0][layer].finish()):
            for block in range(4):
                grads2[layer, block, half] = value[block]
        stages[1][layer].start_one()
    for layer in (1, 0):
        stages[1][layer].start_two()
    for layer in (1, 0):
        for half, value in enumerate(stages[1][layer].finish()):
            for quarter in range(4):
                send_z[half * 4 + quarter, layer] = value[quarter * 16 : (quarter + 1) * 16]
    z_copies = []
    for step in (1, 7, 2, 6, 3, 5, 4):
        other = lax.rem(pack + step, 8)
        z_copies.append(
            pltpu.make_async_remote_copy(
                src_ref=send_z.at[other],
                dst_ref=got_z.at[pack],
                send_sem=z_send.at[step],
                recv_sem=z_recv.at[step],
                device_id=(event, other, tensor),
                device_id_type=MESH,
            )
        )
        z_copies[-1].start()
    got_z[pack] = send_z[pack]
    end_exchange(send_rows, back_rows, send_sem.at[2], recv_sem.at[2])
    wide[...] = back_rows[...].reshape(GROUPS * BLOCK_ROWS, 128).astype(f32)
    total = None
    for k in range(CAP):
        term = dot32(one_hot(picks[k]), joined_rows(wide, k), ((0,), (0,)))
        total = term if total is None else total + term
    row_grad[...] = total.astype(bf16)
    gather.end()
    for copy in z_copies:
        copy.wait()
    total = got_z[0].astype(jnp.float32)
    for source in range(1, 8):
        total = total + got_z[source].astype(jnp.float32)
    enc_grad[...] = total


def hand_over(packed_in, row_in, enc_in, packed_out, row_out, enc_out):
    packed_out[...] = packed_in[...]
    row_out[...] = row_in[...]
    enc_out[...] = enc_in[...]


def shards(
    features,
    dest_owner,
    dest_slot,
    doc_ids,
    enc_weight,
    attn_in,
    attn_out,
    ffn_in,
    ffn_out,
    out_grad,
):
    bf16, f32 = jnp.bfloat16, jnp.float32
    vmem = pl.BlockSpec(memory_space=pltpu.VMEM)
    hbm = pl.BlockSpec(memory_space=pl.ANY)
    dma = pltpu.SemaphoreType.DMA
    packed_out, row_grad, enc_grad = pl.pallas_call(
        step_kernel,
        out_shape=(
            jax.ShapeDtypeStruct((128, 1024), bf16),
            jax.ShapeDtypeStruct((128, 1024), bf16),
            jax.ShapeDtypeStruct((2, 16, 256), f32),
        ),
        in_specs=[vmem] * 5 + [hbm] * 8,
        out_specs=(vmem, vmem, vmem),
        scratch_shapes=[
            pltpu.VMEM((2, 1024, 1024), bf16),
            pltpu.VMEM((4, 2, 4, 2, 128, 256), bf16),
            pltpu.VMEM((4, 2, 8, 2, 64, 256), bf16),
            pltpu.VMEM((4, 4, 2, 2, 16, 1024), bf16),
            pltpu.VMEM((4, 4, 2, 2, 64, 512), bf16),
            pltpu.VMEM((4, 2, 2, 256, 512), bf16),
            pltpu.VMEM((4, 8, 2, 16, 1024), bf16),
            pltpu.VMEM((4, 2, 2, 64, 1024), bf16),
            pltpu.VMEM((128, 1024), f32),
            pltpu.VMEM((GROUPS * BLOCK_ROWS, 128), f32),
            pltpu.VMEM((GROUPS, BLOCK_ROWS, 128), bf16),
            pltpu.VMEM((GROUPS, BLOCK_ROWS, 128), bf16),
            pltpu.VMEM((GROUPS, 1, 128), f32),
            pltpu.VMEM((GROUPS, 1, 128), f32),
            pltpu.VMEM((GROUPS, BLOCK_ROWS, 128), bf16),
            pltpu.VMEM((2, 2, 128, 1024), bf16),
            pltpu.VMEM((2, 2, 128, 1024), bf16),
            pltpu.VMEM((2, 4, 2, 4, 64, 256), bf16),
            pltpu.VMEM((2, 2, 2, 4, 64, 256), bf16),
            pltpu.VMEM((2, 2, 4, 64, 256), bf16),
            pltpu.VMEM((2, 2, 4, 64, 256), bf16),
            pltpu.VMEM((2, 4, 2, 64, 256), bf16),
            pltpu.VMEM((2, 2, 2, 64, 256), bf16),
            pltpu.VMEM((2, 2, 64, 256), bf16),
            pltpu.VMEM((2, 2, 64, 256), bf16),
            pltpu.VMEM((8, 2, 16, 256), bf16),
            pltpu.VMEM((8, 2, 16, 256), bf16),
            pltpu.VMEM((2, 128, 1024), bf16),
            pltpu.VMEM((4, 2, 128, 256), bf16),
            pltpu.VMEM((4, 2, 256, 256), bf16),
            pltpu.VMEM((4, 2, 256, 256), bf16),
            pltpu.VMEM((4, 128, 256), f32),
            pltpu.VMEM((4, 128, 256), f32),
            pltpu.VMEM((4, 4, 128, 256), bf16),
            pltpu.VMEM((4, 4, 128, 256), f32),
            pltpu.VMEM((128, 1024), f32),
            pltpu.VMEM((128, 1024), f32),
            pltpu.VMEM((128, 1024), f32),
            pltpu.VMEM((128, 1024), bf16),
            pltpu.VMEM((128, 256), f32),
            pltpu.VMEM((128, 128), f32),
            pltpu.VMEM((4, 4, 128, 256), bf16),
            pltpu.VMEM((4, 128, 256), bf16),
            pltpu.VMEM((2, 128, 1024), bf16),
            pltpu.VMEM((128, 1024), bf16),
            dma((9,)),
            dma((3,)),
            dma((3,)),
            pltpu.SemaphoreType.REGULAR,
            dma((96,)),
            dma((96,)),
            dma((4,)),
            dma((4,)),
            dma((24,)),
            dma((24,)),
            dma((8,)),
            dma((8,)),
            dma((4,)),
        ],
        compiler_params=pltpu.CompilerParams(
            collective_id=0, has_side_effects=True, vmem_limit_bytes=VMEM_LIMIT
        ),
        name="train_step",
    )(
        features,
        dest_owner.reshape(1, 128),
        dest_slot.reshape(1, 128),
        doc_ids,
        out_grad[0],
        enc_weight,
        attn_in.reshape(4, 4, 2, 128, 256),
        attn_in.reshape(4, 8, 2, 64, 256),
        attn_out.reshape(4, 2, 2, 16, 1024),
        ffn_in.reshape(2, 4, 2, 2, 64, 512),
        ffn_in.reshape(2, 2, 2, 256, 512),
        ffn_out.reshape(2, 8, 2, 16, 1024),
        ffn_out.reshape(2, 2, 2, 64, 1024),
    )
    packed_out, row_grad, enc_grad = pl.pallas_call(
        hand_over,
        out_shape=(
            jax.ShapeDtypeStruct((128, 1024), bf16),
            jax.ShapeDtypeStruct((128, 1024), bf16),
            jax.ShapeDtypeStruct((2, 16, 256), f32),
        ),
        in_specs=[vmem] * 3,
        out_specs=(vmem, vmem, vmem),
        name="hand_over",
    )(packed_out, row_grad, enc_grad)
    return (packed_out[None], row_grad, enc_grad)


def solution(mesh):
    placed = (
        P(("event", "pack", "tensor"), None),
        P(("event", "pack", "tensor")),
        P(("event", "pack", "tensor")),
        P(("event", "pack"), None),
        P(),
        P(None, None, "tensor"),
        P("tensor", None),
        P(None, None, "tensor"),
        P("tensor", None),
        P(("event", "pack"), "tensor", None),
    )
    return jax.shard_map(
        shards,
        mesh=mesh,
        in_specs=placed,
        out_specs=(
            P(("event", "pack"), "tensor", None),
            P(("event", "pack", "tensor"), None),
            P(None, ("event", "pack"), "tensor"),
        ),
        check_vma=False,
    )
```

```python
import jax
import jax.numpy as jnp
from jax import lax
from jax.experimental import pallas as pl
from jax.experimental.pallas import tpu as pltpu
from jax.sharding import PartitionSpec as P

MESH = pl.DeviceIdType.MESH
EPS = 1e-06
GROUPS = 64
CAP = 3
BLOCK_ROWS = CAP * 8
VMEM_LIMIT = 63 * 1024 * 1024
HEAD_SCALE = 64**-0.5


def silu_grad(value):
    sigma = jax.nn.sigmoid(value)
    return sigma * (1.0 + value * (1.0 - sigma))


def norm_rows(rows):
    factor = lax.rsqrt(jnp.mean(rows * rows, axis=-1, keepdims=True) + EPS)
    return (rows * factor, factor)


def norm_back(grad, normed, factor):
    return factor * (grad - normed * jnp.mean(grad * normed, axis=-1, keepdims=True))


def where_am_i():
    return (lax.axis_index("event"), lax.axis_index("pack"), lax.axis_index("tensor"))


def start_exchange(source, target, event, pack, tensor, send_sem, recv_sem, first=1, last=GROUPS):
    me = event * 8 + pack

    def start(step, carry):
        chip = lax.rem(event // 2 + step // 16, 4)
        core = lax.rem(event + step // 8, 2)
        other_pack = lax.rem(pack + step, 8)
        other_event = chip * 2 + core
        pltpu.make_async_remote_copy(
            src_ref=source.at[other_event * 8 + other_pack],
            dst_ref=target.at[me],
            send_sem=send_sem,
            recv_sem=recv_sem,
            device_id=(other_event, other_pack, tensor),
            device_id_type=MESH,
        ).start()
        return carry

    lax.fori_loop(first, last, start, 0)
    if first == 1:
        target[me] = source[me]


def await_bytes(ref, sem):
    pltpu.make_async_copy(ref, ref, sem).wait()


def end_exchange(source, target, send_sem, recv_sem):
    await_bytes(source.at[pl.ds(0, GROUPS - 1)], send_sem)
    await_bytes(target.at[pl.ds(0, GROUPS - 1)], recv_sem)


def dot32(left, right, dims=((1,), (0,))):
    return lax.dot_general(left, right, (dims, ((), ())), preferred_element_type=jnp.float32)


def routing(owner_row):
    rows = jnp.broadcast_to(owner_row, (128, 128))
    columns = rows.T
    earlier = lax.broadcasted_iota(jnp.int32, (128, 128), 0) < lax.broadcasted_iota(
        jnp.int32, (128, 128), 1
    )
    rank = jnp.sum(jnp.where((columns == rows) & earlier, 1.0, 0.0), axis=0, keepdims=True)
    group = lax.broadcasted_iota(jnp.int32, (GROUPS, 128), 0).astype(jnp.float32)
    mine = owner_row == group
    return [mine & (rank == float(k)) for k in range(CAP)]


def one_hot(mask):
    return jnp.where(mask, 1.0, 0.0).astype(jnp.bfloat16)


def spread_rows(wide, k, rows):
    for part in range(8):
        wide[pl.ds(k * 8 + part, GROUPS, stride=BLOCK_ROWS), :] = rows[
            :, part * 128 : (part + 1) * 128
        ]


def joined_rows(wide, k):
    return jnp.concatenate(
        [wide[pl.ds(k * 8 + part, GROUPS, stride=BLOCK_ROWS), :] for part in range(8)], axis=1
    ).astype(jnp.bfloat16)


def silu(value):
    return value * jax.nn.sigmoid(value)


class Halving:
    def __init__(self, blocks, first, second, outgoing, sems, base, index, device):
        self.blocks, self.first, self.second, self.outgoing = blocks, first, second, outgoing
        self.sems, self.base, self.index = sems, base, index
        near = index + 1 - 2 * lax.rem(index, 2)
        self.other = (near, 3 - index)
        self.far = lax.rem(index + 2, 4)
        self.device = device

    def copy(self, source, target, number, half_partner):
        send, recv = self.sems
        return pltpu.make_async_remote_copy(
            src_ref=source,
            dst_ref=target,
            send_sem=send.at[self.base + number],
            recv_sem=recv.at[self.base + number],
            device_id=self.device(half_partner),
            device_id_type=MESH,
        )

    def round_one(self):
        copies = []
        for half in range(2):
            partner = self.other[half]
            for slot, block in enumerate((partner, self.far)):
                copies.append(
                    self.copy(
                        self.blocks.at[block, half],
                        self.first.at[half, slot],
                        half * 2 + slot,
                        partner,
                    )
                )
        return copies

    def round_two(self):
        return [
            self.copy(self.outgoing.at[half], self.second.at[half], 4 + half, self.other[1 - half])
            for half in range(2)
        ]

    def start_one(self):
        for copy in self.round_one():
            copy.start()

    def start_two(self):
        for copy in self.round_one():
            copy.wait()
        for half in range(2):
            block = self.other[1 - half]
            self.outgoing[half] = (
                self.blocks[block, half].astype(jnp.float32)
                + self.first[half, 1].astype(jnp.float32)
            ).astype(jnp.bfloat16)
        for copy in self.round_two():
            copy.start()

    def finish(self):
        for copy in self.round_two():
            copy.wait()
        return [
            (
                self.blocks[self.index, half].astype(jnp.float32)
                + self.first[half, 0].astype(jnp.float32)
                + self.second[half].astype(jnp.float32)
            ).astype(jnp.bfloat16)
            for half in range(2)
        ]


class Gather:
    def __init__(self, send, recv, event, pack, tensor):
        self.send, self.recv = send, recv
        self.event, self.pack, self.tensor = event, pack, tensor
        self.core = lax.rem(event, 2)
        self.used = 0
        self.started = []
        self.partner = (event + 1 - 2 * self.core, pack, tensor)
        self.pair_started = []

    def copy(self, source, target, device):
        number = self.used
        self.used += 1
        copy = pltpu.make_async_remote_copy(
            src_ref=source,
            dst_ref=target,
            send_sem=self.send.at[number],
            recv_sem=self.recv.at[number],
            device_id=device,
            device_id_type=MESH,
        )
        copy.start()
        self.started.append(copy)
        return copy

    def along_tensor(self, shift):
        return (self.event, self.pack, lax.rem(self.tensor + shift + 4, 4))

    def along_x(self, shift):
        return (lax.rem(self.event + 2 * shift + 8, 8), self.pack, self.tensor)

    def along_z(self, shift):
        return (self.event, lax.rem(self.pack + shift + 8, 8), self.tensor)

    def to_pair(self, region, name):
        self.pair_started.append((name, self.copy(region, region, self.partner)))

    def await_pair(self, names):
        for name, copy in self.pair_started:
            if name in names:
                copy.wait_recv()

    def end(self):
        for copy in self.started:
            copy.wait_send()


class TensorRing:
    def __init__(self, gather, name, own, region, halves):
        self.gather, self.name, self.own = gather, name, own
        self.region, self.halves = region, halves

    def start(self):
        device = self.gather.along_tensor
        self.near = [
            self.gather.copy(self.own, self.region(2), device(1)),
            self.gather.copy(self.own, self.region(1), device(-1)),
        ]

    def relay(self):
        for copy in self.near:
            copy.wait_recv()
        device = self.gather.along_tensor
        plus, minus = self.halves
        self.far = []
        if plus is not False:
            self.far.append(self.gather.copy(self.region(2, plus), self.region(3, plus), device(1)))
        if minus is not False:
            self.far.append(
                self.gather.copy(self.region(1, minus), self.region(3, minus), device(-1))
            )
        self.gather.to_pair(self.region(pl.ds(1, 2)), self.name)

    def end(self):
        for copy in self.far:
            copy.wait_recv()
        self.gather.to_pair(self.region(pl.ds(3, 1)), self.name)


class SideRing:
    def __init__(self, gather, name, size, index, device, region, halves):
        self.gather, self.name, self.size, self.index = gather, name, size, index
        self.device, self.region, self.halves = device, region, halves
        self.step = 0
        self.flying = None

    def block(self, shift, half=None):
        return self.region(lax.rem(self.index + shift + self.size, self.size), half)

    def start(self):
        block = self.block(0)
        self.flying = [
            self.gather.copy(block, block, self.device(1)),
            self.gather.copy(block, block, self.device(-1)),
        ]
        self.step = 1

    def advance(self):
        for copy in self.flying:
            copy.wait_recv()
        step = self.step
        last = step == self.size // 2
        forward = []
        if not last:
            halves = (None, None) if step + 1 < self.size // 2 else self.halves
            for sign, half in zip((1, -1), halves):
                if half is not False:
                    block = self.block(-sign * step, half)
                    forward.append(self.gather.copy(block, block, self.device(sign)))
            for sign in (1, -1):
                self.gather.to_pair(self.block(-sign * step), self.name)
        else:
            self.gather.to_pair(self.block(step), self.name)
        self.flying = forward
        self.step = step + 1


def masks(documents, tensor):
    own = documents[:, pl.ds(pl.multiple_of(tensor * 128, 128), 128)].astype(jnp.float32)
    before = documents[
        :, pl.ds(pl.multiple_of(lax.rem(tensor + 3, 4) * 128, 128), 128)
    ].astype(jnp.float32)
    before = before - jnp.where(tensor == 0, 1000.0, 0.0)
    mine = jnp.broadcast_to(own, (128, 128)).T
    row = lax.broadcasted_iota(jnp.int32, (128, 128), 0)
    column = lax.broadcasted_iota(jnp.int32, (128, 128), 1)
    allowed = jnp.concatenate(
        [
            jnp.where(mine == before, 1.0, 0.0),
            jnp.where((mine == own) & (column <= row), 1.0, 0.0),
        ],
        axis=1,
    )
    root = jnp.sqrt(jnp.sum(allowed, axis=1, keepdims=True))
    return (allowed, root)


def by_parity(value):
    first = lax.rem(lax.broadcasted_iota(jnp.int32, value.shape, 1), 128) < 64
    return (
        jnp.where(first, value, 0.0).astype(jnp.bfloat16),
        jnp.where(first, 0.0, value).astype(jnp.bfloat16),
    )


def rounded(value):
    return value.astype(jnp.bfloat16).astype(jnp.float32)


def step_kernel(
    features,
    owner,
    slot,
    documents,
    out_grad,
    enc_hbm,
    first_hbm,
    second_hbm,
    attn_out_hbm,
    gate_hbm,
    up_hbm,
    down_z_hbm,
    down_t_hbm,
    packed_hbm,
    row_hbm,
    enc_grad,
    packed_out,
    row_grad,
    enc,
    first,
    second,
    attn_out,
    gate_in,
    up_in,
    down_z,
    down_t,
    preact,
    wide,
    send_rows,
    got_rows,
    send_slots,
    got_slots,
    back_rows,
    acts,
    cots,
    grads,
    firsts,
    seconds,
    outs,
    grads2,
    firsts2,
    seconds2,
    outs2,
    send_z,
    got_z,
    normed,
    query,
    keys,
    values,
    gates,
    attended,
    weights,
    slopes,
    slopes16,
    total_a,
    total_b,
    residual,
    normed2,
    allowed_ref,
    root_ref,
    d_proj,
    gated,
    halo_send,
    halo_got,
    load_sem,
    send_sem,
    recv_sem,
    ready_sem,
    gather_send,
    gather_recv,
    pair_send,
    pair_recv,
    half_send,
    half_recv,
    z_send,
    z_recv,
    halo_sem,
):
    event, pack, tensor = where_am_i()
    core = lax.rem(event, 2)
    chip_x = event // 2
    partner = (event + 1 - 2 * core, pack, tensor)
    bf16, f32 = jnp.bfloat16, jnp.float32
    barrier = pltpu.get_barrier_semaphore()
    loads = []
    for number, (source, target) in enumerate(
        (
            (enc_hbm.at[0], enc.at[0]),
            (enc_hbm.at[1], enc.at[1]),
            (first_hbm.at[pl.ds(0, 2)], first.at[0]),
            (second_hbm.at[pl.ds(2, 2)], second.at[0]),
            (attn_out_hbm, attn_out.at[0]),
            (gate_hbm.at[0], gate_in.at[0]),
            (up_hbm.at[1], up_in.at[0]),
            (down_z_hbm.at[0], down_z.at[0]),
            (down_t_hbm.at[1], down_t.at[0]),
        )
    ):
        load = pltpu.make_async_copy(source, target, load_sem.at[number])
        load.start()
        loads.append(load)
    for step in range(1, 8):
        for device in (
            (event, lax.rem(pack + step, 8), tensor),
            (lax.rem(event + step, 8), pack, tensor),
        ):
            pl.semaphore_signal(barrier, inc=1, device_id=device, device_id_type=MESH)
    for step in (1, 3):
        pl.semaphore_signal(
            barrier,
            inc=1,
            device_id=(event, pack, lax.rem(tensor + step, 4)),
            device_id_type=MESH,
        )
    picks = routing(owner[...].astype(f32))
    slot_row = slot[...].astype(f32) + 1.0
    lane = lax.broadcasted_iota(jnp.int32, (GROUPS, 128), 1)
    slots = jnp.full((GROUPS, 128), -1.0, f32)
    for k in range(CAP):
        value = jnp.sum(jnp.where(picks[k], slot_row, 0.0), axis=1, keepdims=True) - 1.0
        slots = jnp.where(lane == k, value, slots)
    send_slots[:, 0, :] = slots
    for k in range(CAP):
        spread_rows(wide, k, dot32(one_hot(picks[k]), features[...]))
    send_rows[...] = wide[...].astype(bf16).reshape(GROUPS, BLOCK_ROWS, 128)
    pl.semaphore_wait(barrier, 16)
    for step in range(1, 8):
        pl.semaphore_signal(
            ready_sem,
            inc=1,
            device_id=(lax.rem(event + step, 8), pack, tensor),
            device_id_type=MESH,
        )

    gather = Gather(gather_send, gather_recv, event, pack, tensor)
    whole = slice(None)
    low, high = pl.ds(0, 1), pl.ds(1, 1)
    foreign = pl.ds(1, 3)

    def part_of(half):
        return whole if half is None else half

    def first_at(where, index, half=None):
        return first.at[where, part_of(half), index, core]

    def second_at(where, index, half=None):
        return second.at[where, part_of(half), index, core]

    def attn_out_at(where, index, half=None):
        return attn_out.at[where, index, core, part_of(half)]

    def gate_at(where, index, half=None):
        return gate_in.at[where, index, core, part_of(half)]

    def down_z_at(where, index, half=None):
        return down_z.at[where, index, core]

    def up_at(where, half=None):
        return up_in.at[where, core, part_of(half)]

    def down_t_at(where, half=None):
        return down_t.at[where, core, part_of(half)]

    def slice_ring(name, own, region, index, halves):
        return TensorRing(
            gather, name, own, lambda where, half=None: region(where, index, half), halves
        )

    t_first = slice_ring(
        "attn", first_hbm.at[pl.ds(0, 2), chip_x, core], first_at, chip_x, (low, high)
    )
    t_second = slice_ring(
        "attn", second_hbm.at[pl.ds(2, 2), pack, core], second_at, pack, (low, high)
    )
    t_out = slice_ring("out", attn_out_hbm.at[chip_x, core], attn_out_at, chip_x, (low, high))
    t_gate = slice_ring("ffn", gate_hbm.at[0, chip_x, core], gate_at, chip_x, (low, high))
    t_down = slice_ring("ffn", down_z_hbm.at[0, pack, core], down_z_at, pack, (False, None))
    t_up = TensorRing(gather, "ffn", up_hbm.at[1, core], up_at, (low, high))
    t_last = TensorRing(gather, "ffn", down_t_hbm.at[1, core], down_t_at, (low, high))

    def side_ring(name, axis, region, halves):
        size, index, device = (
            (4, chip_x, gather.along_x) if axis == "x" else (8, pack, gather.along_z)
        )
        return SideRing(
            gather,
            name,
            size,
            index,
            device,
            lambda number, half=None: region(foreign, number, half),
            halves,
        )

    x_first = side_ring("attn", "x", first_at, (low, high))
    z_second = side_ring("attn", "z", second_at, (low, high))
    x_out = side_ring("out", "x", attn_out_at, (low, high))
    x_gate = side_ring("ffn", "x", gate_at, (low, high))
    z_down = side_ring("ffn", "z", down_z_at, (None, False))

    t_second.start()
    t_first.start()
    t_down.start()
    t_out.start()
    t_gate.start()
    pl.semaphore_wait(ready_sem, 7)
    start_exchange(send_slots, got_slots, event, pack, tensor, send_sem.at[0], recv_sem.at[0])
    start_exchange(send_rows, got_rows, event, pack, tensor, send_sem.at[1], recv_sem.at[1])
    t_second.relay()
    t_first.relay()
    t_up.start()
    t_down.relay()
    t_second.end()
    z_second.start()
    t_out.relay()
    t_first.end()
    x_first.start()
    t_gate.relay()
    allowed, root = masks(documents, tensor)
    allowed_ref[...] = allowed
    root_ref[...] = jnp.broadcast_to(root, (128, 128))

    def pair_copy(number, array):
        return pltpu.make_async_remote_copy(
            src_ref=array.at[0],
            dst_ref=array.at[1],
            send_sem=pair_send.at[number],
            recv_sem=pair_recv.at[number],
            device_id=partner,
            device_id_type=MESH,
        )

    end_exchange(send_slots, got_slots, send_sem.at[0], recv_sem.at[0])
    end_exchange(send_rows, got_rows, send_sem.at[1], recv_sem.at[1])
    wide[...] = got_rows[...].reshape(GROUPS * BLOCK_ROWS, 128).astype(f32)
    turned = jnp.concatenate([got_slots[:, 0, :], jnp.full((GROUPS, 128), -1.0, f32)], axis=0).T
    place = lax.broadcasted_iota(jnp.int32, (128, GROUPS), 0).astype(f32)
    total = None
    for k in range(CAP):
        pick = one_hot(turned[k : k + 1, :GROUPS] == place)
        term = dot32(pick, joined_rows(wide, k))
        total = term if total is None else total + term
    rows = total.astype(bf16)
    for load in loads[:2]:
        load.wait()
    pre = dot32(rows, enc[0])
    preact[...] = pre
    act = silu(pre).astype(bf16)
    quarter = rounded(dot32(act, enc[1]))
    normed_f, factor1 = norm_rows(quarter)
    halo_send[0] = normed_f.astype(bf16)
    normed[1] = normed_f.astype(bf16)
    residual[...] = quarter

    def halo_copy(number, target, shift):
        return pltpu.make_async_remote_copy(
            src_ref=halo_send.at[number],
            dst_ref=target,
            send_sem=halo_sem.at[number],
            recv_sem=halo_sem.at[2 + number],
            device_id=(event, pack, lax.rem(tensor + shift, 4)),
            device_id_type=MESH,
        )

    halo = halo_copy(0, normed.at[0], 1)
    halo.start()
    acts[0, 0] = rows
    acts[1, 0] = act
    act_copies = [pair_copy(layer, acts.at[layer]) for layer in range(2)]
    for copy in act_copies:
        copy.start()
    t_last.start()
    z_second.advance()
    x_first.advance()
    t_down.end()
    z_down.start()
    t_out.end()
    x_out.start()
    z_second.advance()
    t_gate.end()
    x_gate.start()
    t_up.relay()
    x_first.advance()
    z_second.advance()
    z_down.advance()
    for load in loads[2:4]:
        load.wait()
    halo.wait()
    own_rows = normed[1]
    all_rows = normed[...].reshape(256, 1024)
    total_a[...] = quarter

    def matrix(slot_index, number):
        source = first if number < 2 else second
        return source[slot_index, number % 2].reshape(1024, 256)

    def attend(slot_index):
        query_f = rounded(dot32(own_rows, matrix(slot_index, 0)))
        gate = rounded(dot32(own_rows, matrix(slot_index, 3)))
        keys_f = rounded(dot32(all_rows, matrix(slot_index, 1)))
        values_f = rounded(dot32(all_rows, matrix(slot_index, 2)))
        gates[slot_index] = gate
        sides = []
        for ref, value in ((query, query_f), (keys, keys_f), (values, values_f)):
            pieces = by_parity(value)
            for parity in range(2):
                ref[slot_index, parity] = pieces[parity]
            sides.append(pieces)
        parts = []
        allowed = allowed_ref[...] > 0.5
        for pair in range(2):
            columns = slice(pair * 128, (pair + 1) * 128)
            part = None
            for parity in range(2):
                scores = (
                    dot32(sides[0][parity][:, columns], sides[1][parity][:, columns], ((1,), (1,)))
                    * HEAD_SCALE
                )
                sigma = jax.nn.sigmoid(scores)
                weight = jnp.where(allowed, scores * sigma, 0.0).astype(bf16)
                weights[slot_index, pair * 2 + parity] = weight
                slopes[slot_index, pair * 2 + parity] = jnp.where(
                    allowed, sigma * (1.0 + scores * (1.0 - sigma)), 0.0
                )
                term = dot32(weight, sides[2][parity][:, columns])
                part = term if part is None else part + term
            parts.append(part)
        result = jnp.concatenate(parts, axis=1) / root_ref[:, 0:1]
        attended[slot_index] = result
        gated[slot_index] = (result * silu(gate)).astype(bf16)

    attend(0)
    z_second.advance()
    gather.await_pair(("attn",))
    x_out.advance()
    z_down.advance()
    attend(1)
    x_gate.advance()
    t_last.relay()
    attend(2)
    z_down.advance()
    x_out.advance()
    attend(3)
    gather.await_pair(("out",))
    loads[4].wait()
    for slot_index in range(4):
        total_a[...] += rounded(
            dot32(gated[slot_index], attn_out[slot_index].reshape(256, 1024))
        )
    resid = rounded(total_a[...])
    normed2_f, factor2 = norm_rows(resid)
    normed2[...] = normed2_f.astype(bf16)
    total_a[...] = resid
    total_b[...] = jnp.zeros((128, 1024), f32)

    def feed(slot_index, carry):
        rows = normed2[...]
        gate = dot32(rows, gate_in[slot_index].reshape(1024, 512))
        upper = dot32(rows, up_in[slot_index].reshape(1024, 512))
        sigma = jax.nn.sigmoid(gate)
        active = gate * sigma
        down = (down_z[slot_index].reshape(256, 1024), down_t[slot_index].reshape(256, 1024))
        hidden = (active * upper).astype(bf16)
        total_a[...] += rounded(dot32(hidden[:, :256], down[0]) + dot32(hidden[:, 256:], down[1]))
        d_hidden = jnp.concatenate(
            [dot32(out_grad[...], part, ((1,), (1,))) for part in down], axis=1
        )
        d_gate = (d_hidden * upper * (sigma * (1.0 + gate * (1.0 - sigma)))).astype(bf16)
        d_upper = (d_hidden * active).astype(bf16)
        total_b[...] += rounded(
            dot32(d_gate, gate_in[slot_index].reshape(1024, 512), ((1,), (1,)))
            + dot32(d_upper, up_in[slot_index].reshape(1024, 512), ((1,), (1,)))
        )
        return carry

    z_down.advance()
    x_gate.advance()
    t_up.end()
    t_last.end()
    gather.await_pair(("ffn",))
    for load in loads[5:]:
        load.wait()
    lax.fori_loop(0, 4, feed, 0)
    packed_out[...] = total_a[...].astype(bf16)
    stores = [
        pltpu.make_async_copy(packed_out, packed_hbm, load_sem.at[0]),
        pltpu.make_async_copy(row_grad, row_hbm, load_sem.at[1]),
    ]
    stores[0].start()
    d_resid = (
        out_grad[...].astype(f32) + norm_back(total_b[...], normed2_f, factor2)
    ).astype(bf16)
    total_a[...] = jnp.zeros((128, 1024), f32)
    total_b[...] = jnp.zeros((128, 1024), f32)

    def attend_back(slot_index, carry):
        gate = gates[slot_index]
        d_gated = dot32(d_resid, attn_out[slot_index].reshape(256, 1024), ((1,), (1,)))
        sigma = jax.nn.sigmoid(gate)
        d_attended = by_parity(d_gated * (gate * sigma) / root_ref[:, 0:1])
        d_gate = (
            d_gated * attended[slot_index] * (sigma * (1.0 + gate * (1.0 - sigma)))
        ).astype(bf16)
        d_parts = [[], []]
        for pair in range(2):
            columns = slice(pair * 128, (pair + 1) * 128)
            sums = [None, None]
            for parity in range(2):
                head = pair * 2 + parity
                d_side = d_attended[parity][:, columns]
                d_weights = dot32(d_side, values[slot_index, parity, :, columns], ((1,), (1,)))
                d_scores = (d_weights * slopes[slot_index, head]).astype(bf16)
                slopes16[slot_index, head] = d_scores
                terms = (
                    dot32(d_scores, query[slot_index, parity, :, columns], ((0,), (0,))),
                    dot32(weights[slot_index, head], d_side, ((0,), (0,))),
                )
                for number, term in enumerate(terms):
                    sums[number] = term if sums[number] is None else sums[number] + term
            d_parts[0].append(sums[0] * HEAD_SCALE)
            d_parts[1].append(sums[1])
        d_keys, d_values = (
            jnp.concatenate(parts, axis=1).astype(bf16) for parts in d_parts
        )
        for number, value in enumerate((d_keys[128:], d_values[128:], d_gate)):
            d_proj[slot_index, number] = value
        total_b[...] += dot32(d_keys[:128], matrix(slot_index, 1), ((1,), (1,))) + dot32(
            d_values[:128], matrix(slot_index, 2), ((1,), (1,))
        )
        return carry

    lax.fori_loop(0, 4, attend_back, 0)
    halo_send[1] = total_b[...].astype(bf16)
    halo_back = halo_copy(1, halo_got, 3)
    halo_back.start()

    def project_back(slot_index, carry):
        parts = []
        for pair in range(2):
            columns = slice(pair * 128, (pair + 1) * 128)
            parts.append(
                (
                    dot32(slopes16[slot_index, pair * 2], keys[slot_index, 0, :, columns])
                    + dot32(slopes16[slot_index, pair * 2 + 1], keys[slot_index, 1, :, columns])
                )
                * HEAD_SCALE
            )
        d_query = jnp.concatenate(parts, axis=1).astype(bf16)
        total_a[...] += dot32(d_query, matrix(slot_index, 0), ((1,), (1,))) + sum(
            dot32(d_proj[slot_index, number - 1], matrix(slot_index, number), ((1,), (1,)))
            for number in range(1, 4)
        )
        return carry

    lax.fori_loop(0, 4, project_back, 0)
    halo_back.wait()
    d_normed = total_a[...] + halo_got[...].astype(f32)
    normed_f, factor1 = norm_rows(residual[...])
    d_quarter = (d_resid.astype(f32) + norm_back(d_normed, normed_f, factor1)).astype(bf16)
    cots[1, 0] = d_quarter
    cot_copies = [pair_copy(2 + layer, cots.at[layer]) for layer in range(2)]
    cot_copies[1].start()
    cots[0, 0] = (
        dot32(d_quarter, enc[1], ((1,), (1,))) * silu_grad(preact[...])
    ).astype(bf16)
    cot_copies[0].start()
    for copy in act_copies:
        copy.wait()

    def tensor_device(index):
        return (event, pack, index)

    def chip_device(index):
        return (index * 2 + core, pack, tensor)

    rings = ((tensor, tensor_device), (chip_x, chip_device))
    stages = [[], []]
    for unit in range(4):
        for stage, refs in enumerate(
            ((grads, firsts, seconds, outs), (grads2, firsts2, seconds2, outs2))
        ):
            index, device = rings[stage if unit < 3 else 1 - stage]
            stages[stage].append(
                Halving(
                    *(ref.at[unit] for ref in refs),
                    (half_send, half_recv),
                    (stage * 4 + unit) * 6,
                    index,
                    device,
                )
            )
    for layer in (1, 0):
        cot_copies[layer].wait()
        cot = cots[layer].reshape(256, 1024)
        units = (0, 1) if layer == 1 else (2, 3)
        for chip in range(4):
            columns = pl.ds(pl.multiple_of((chip * 2 + core) * 128, 128), 128)
            act = acts[layer, :, :, columns].reshape(256, 128)
            term = dot32(act, cot, ((0,), (0,))).astype(bf16)
            for block in range(4):
                for half in range(2):
                    for part in range(2):
                        low_row = half * 64 + part * 32
                        piece = term[low_row : low_row + 32, block * 256 : (block + 1) * 256]
                        if units[part] < 3:
                            grads[units[part], block, half, chip] = piece
                        else:
                            grads[units[part], chip, half, block] = piece
        for unit in units:
            stages[0][unit].start_one()
    lane = lax.broadcasted_iota(jnp.int32, (GROUPS, 128), 1).astype(jnp.float32)
    for k in range(CAP):
        chosen = one_hot(got_slots[:, 0, k : k + 1] == lane)
        spread_rows(wide, k, dot32(chosen, d_quarter))
    send_rows[...] = wide[...].astype(bf16).reshape(GROUPS, BLOCK_ROWS, 128)
    start_exchange(send_rows, back_rows, event, pack, tensor, send_sem.at[2], recv_sem.at[2])
    for unit in range(4):
        stages[0][unit].start_two()
    for unit in range(4):
        for half, value in enumerate(stages[0][unit].finish()):
            for block in range(4):
                grads2[unit, block, half] = value[block]
        stages[1][unit].start_one()
    for unit in range(4):
        stages[1][unit].start_two()
    for unit in range(4):
        for half, value in enumerate(stages[1][unit].finish()):
            for number in range(2):
                send_z[half * 4 + unit % 2 * 2 + number, 1 - unit // 2] = value[
                    number * 16 : (number + 1) * 16
                ]
    z_copies = []
    for step in (1, 7, 2, 6, 3, 5, 4):
        other = lax.rem(pack + step, 8)
        z_copies.append(
            pltpu.make_async_remote_copy(
                src_ref=send_z.at[other],
                dst_ref=got_z.at[pack],
                send_sem=z_send.at[step],
                recv_sem=z_recv.at[step],
                device_id=(event, other, tensor),
                device_id_type=MESH,
            )
        )
        z_copies[-1].start()
    got_z[pack] = send_z[pack]
    end_exchange(send_rows, back_rows, send_sem.at[2], recv_sem.at[2])
    wide[...] = back_rows[...].reshape(GROUPS * BLOCK_ROWS, 128).astype(f32)
    total = None
    for k in range(CAP):
        term = dot32(one_hot(picks[k]), joined_rows(wide, k), ((0,), (0,)))
        total = term if total is None else total + term
    row_grad[...] = total.astype(bf16)
    stores[1].start()
    gather.end()
    for copy in z_copies:
        copy.wait()
    total = got_z[0].astype(jnp.float32)
    for source in range(1, 8):
        total = total + got_z[source].astype(jnp.float32)
    enc_grad[...] = total
    for store in stores:
        store.wait()


def hand_over(packed_in, row_in, enc_in, packed_out, row_out, enc_out):
    packed_out[...] = packed_in[...]
    row_out[...] = row_in[...]
    enc_out[...] = enc_in[...]


def shards(
    features,
    dest_owner,
    dest_slot,
    doc_ids,
    enc_weight,
    attn_in,
    attn_out,
    ffn_in,
    ffn_out,
    out_grad,
):
    bf16, f32 = jnp.bfloat16, jnp.float32
    vmem = pl.BlockSpec(memory_space=pltpu.VMEM)
    hbm = pl.BlockSpec(memory_space=pl.ANY)
    dma = pltpu.SemaphoreType.DMA
    packed_out, row_grad, enc_grad = pl.pallas_call(
        step_kernel,
        out_shape=(
            jax.ShapeDtypeStruct((128, 1024), bf16),
            jax.ShapeDtypeStruct((128, 1024), bf16),
            jax.ShapeDtypeStruct((2, 16, 256), f32),
        ),
        in_specs=[vmem] * 5 + [hbm] * 8,
        out_specs=(hbm, hbm, vmem),
        scratch_shapes=[
            pltpu.VMEM((128, 1024), bf16),
            pltpu.VMEM((128, 1024), bf16),
            pltpu.VMEM((2, 1024, 1024), bf16),
            pltpu.VMEM((4, 2, 4, 2, 128, 256), bf16),
            pltpu.VMEM((4, 2, 8, 2, 64, 256), bf16),
            pltpu.VMEM((4, 4, 2, 2, 16, 1024), bf16),
            pltpu.VMEM((4, 4, 2, 2, 64, 512), bf16),
            pltpu.VMEM((4, 2, 2, 256, 512), bf16),
            pltpu.VMEM((4, 8, 2, 16, 1024), bf16),
            pltpu.VMEM((4, 2, 2, 64, 1024), bf16),
            pltpu.VMEM((128, 1024), f32),
            pltpu.VMEM((GROUPS * BLOCK_ROWS, 128), f32),
            pltpu.VMEM((GROUPS, BLOCK_ROWS, 128), bf16),
            pltpu.VMEM((GROUPS, BLOCK_ROWS, 128), bf16),
            pltpu.VMEM((GROUPS, 1, 128), f32),
            pltpu.VMEM((GROUPS, 1, 128), f32),
            pltpu.VMEM((GROUPS, BLOCK_ROWS, 128), bf16),
            pltpu.VMEM((2, 2, 128, 1024), bf16),
            pltpu.VMEM((2, 2, 128, 1024), bf16),
            pltpu.VMEM((4, 4, 2, 4, 32, 256), bf16),
            pltpu.VMEM((4, 2, 2, 4, 32, 256), bf16),
            pltpu.VMEM((4, 2, 4, 32, 256), bf16),
            pltpu.VMEM((4, 2, 4, 32, 256), bf16),
            pltpu.VMEM((4, 4, 2, 32, 256), bf16),
            pltpu.VMEM((4, 2, 2, 32, 256), bf16),
            pltpu.VMEM((4, 2, 32, 256), bf16),
            pltpu.VMEM((4, 2, 32, 256), bf16),
            pltpu.VMEM((8, 2, 16, 256), bf16),
            pltpu.VMEM((8, 2, 16, 256), bf16),
            pltpu.VMEM((2, 128, 1024), bf16),
            pltpu.VMEM((4, 2, 128, 256), bf16),
            pltpu.VMEM((4, 2, 256, 256), bf16),
            pltpu.VMEM((4, 2, 256, 256), bf16),
            pltpu.VMEM((4, 128, 256), f32),
            pltpu.VMEM((4, 128, 256), f32),
            pltpu.VMEM((4, 4, 128, 256), bf16),
            pltpu.VMEM((4, 4, 128, 256), f32),
            pltpu.VMEM((4, 4, 128, 256), bf16),
            pltpu.VMEM((128, 1024), f32),
            pltpu.VMEM((128, 1024), f32),
            pltpu.VMEM((128, 1024), f32),
            pltpu.VMEM((128, 1024), bf16),
            pltpu.VMEM((128, 256), f32),
            pltpu.VMEM((128, 128), f32),
            pltpu.VMEM((4, 3, 128, 256), bf16),
            pltpu.VMEM((4, 128, 256), bf16),
            pltpu.VMEM((2, 128, 1024), bf16),
            pltpu.VMEM((128, 1024), bf16),
            dma((9,)),
            dma((3,)),
            dma((3,)),
            pltpu.SemaphoreType.REGULAR,
            dma((96,)),
            dma((96,)),
            dma((4,)),
            dma((4,)),
            dma((48,)),
            dma((48,)),
            dma((8,)),
            dma((8,)),
            dma((4,)),
        ],
        compiler_params=pltpu.CompilerParams(
            collective_id=0, has_side_effects=True, vmem_limit_bytes=VMEM_LIMIT
        ),
        name="train_step",
    )(
        features,
        dest_owner.reshape(1, 128),
        dest_slot.reshape(1, 128),
        doc_ids,
        out_grad[0],
        enc_weight,
        attn_in.reshape(4, 4, 2, 128, 256),
        attn_in.reshape(4, 8, 2, 64, 256),
        attn_out.reshape(4, 2, 2, 16, 1024),
        ffn_in.reshape(2, 4, 2, 2, 64, 512),
        ffn_in.reshape(2, 2, 2, 256, 512),
        ffn_out.reshape(2, 8, 2, 16, 1024),
        ffn_out.reshape(2, 2, 2, 64, 1024),
    )
    packed_out, row_grad, enc_grad = pl.pallas_call(
        hand_over,
        out_shape=(
            jax.ShapeDtypeStruct((128, 1024), bf16),
            jax.ShapeDtypeStruct((128, 1024), bf16),
            jax.ShapeDtypeStruct((2, 16, 256), f32),
        ),
        in_specs=[vmem] * 3,
        out_specs=(vmem, vmem, vmem),
        name="hand_over",
    )(packed_out, row_grad, enc_grad)
    return (packed_out[None], row_grad, enc_grad)


def solution(mesh):
    placed = (
        P(("event", "pack", "tensor"), None),
        P(("event", "pack", "tensor")),
        P(("event", "pack", "tensor")),
        P(("event", "pack"), None),
        P(),
        P(None, None, "tensor"),
        P("tensor", None),
        P(None, None, "tensor"),
        P("tensor", None),
        P(("event", "pack"), "tensor", None),
    )
    return jax.shard_map(
        shards,
        mesh=mesh,
        in_specs=placed,
        out_specs=(
            P(("event", "pack"), "tensor", None),
            P(("event", "pack", "tensor"), None),
            P(None, ("event", "pack"), "tensor"),
        ),
        check_vma=False,
    )
```

```python
import jax
import jax.numpy as jnp
from jax import lax
from jax.experimental import pallas as pl
from jax.experimental.pallas import tpu as pltpu
from jax.sharding import PartitionSpec as P

MESH = pl.DeviceIdType.MESH
EPS = 1e-06
GROUPS = 64
CAP = 3
BLOCK_ROWS = CAP * 8
VMEM_LIMIT = 63 * 1024 * 1024
HEAD_SCALE = 64**-0.5


def silu_grad(value):
    sigma = jax.nn.sigmoid(value)
    return sigma * (1.0 + value * (1.0 - sigma))


def norm_rows(rows):
    factor = lax.rsqrt(jnp.mean(rows * rows, axis=-1, keepdims=True) + EPS)
    return (rows * factor, factor)


def norm_back(grad, normed, factor):
    return factor * (grad - normed * jnp.mean(grad * normed, axis=-1, keepdims=True))


def where_am_i():
    return (lax.axis_index("event"), lax.axis_index("pack"), lax.axis_index("tensor"))


def start_exchange(source, target, event, pack, tensor, send_sem, recv_sem, first=1, last=GROUPS):
    me = event * 8 + pack

    def start(step, carry):
        chip = lax.rem(event // 2 + step // 16, 4)
        core = lax.rem(event + step // 8, 2)
        other_pack = lax.rem(pack + step, 8)
        other_event = chip * 2 + core
        pltpu.make_async_remote_copy(
            src_ref=source.at[other_event * 8 + other_pack],
            dst_ref=target.at[me],
            send_sem=send_sem,
            recv_sem=recv_sem,
            device_id=(other_event, other_pack, tensor),
            device_id_type=MESH,
        ).start()
        return carry

    lax.fori_loop(first, last, start, 0)
    if first == 1:
        target[me] = source[me]


def await_bytes(ref, sem):
    pltpu.make_async_copy(ref, ref, sem).wait()


def end_exchange(source, target, send_sem, recv_sem):
    await_bytes(source.at[pl.ds(0, GROUPS - 1)], send_sem)
    await_bytes(target.at[pl.ds(0, GROUPS - 1)], recv_sem)


def dot32(left, right, dims=((1,), (0,))):
    return lax.dot_general(left, right, (dims, ((), ())), preferred_element_type=jnp.float32)


def routing(owner_row):
    rows = jnp.broadcast_to(owner_row, (128, 128))
    columns = rows.T
    earlier = lax.broadcasted_iota(jnp.int32, (128, 128), 0) < lax.broadcasted_iota(
        jnp.int32, (128, 128), 1
    )
    rank = jnp.sum(jnp.where((columns == rows) & earlier, 1.0, 0.0), axis=0, keepdims=True)
    group = lax.broadcasted_iota(jnp.int32, (GROUPS, 128), 0).astype(jnp.float32)
    mine = owner_row == group
    return [mine & (rank == float(k)) for k in range(CAP)]


def one_hot(mask):
    return jnp.where(mask, 1.0, 0.0).astype(jnp.bfloat16)


def spread_rows(wide, k, rows):
    for part in range(8):
        wide[pl.ds(k * 8 + part, GROUPS, stride=BLOCK_ROWS), :] = rows[
            :, part * 128 : (part + 1) * 128
        ]


def joined_rows(wide, k):
    return jnp.concatenate(
        [wide[pl.ds(k * 8 + part, GROUPS, stride=BLOCK_ROWS), :] for part in range(8)], axis=1
    ).astype(jnp.bfloat16)


def silu(value):
    return value * jax.nn.sigmoid(value)


class Halving:
    def __init__(self, blocks, first, second, outgoing, sems, base, index, device):
        self.blocks, self.first, self.second, self.outgoing = blocks, first, second, outgoing
        self.sems, self.base, self.index = sems, base, index
        near = index + 1 - 2 * lax.rem(index, 2)
        self.other = (near, 3 - index)
        self.far = lax.rem(index + 2, 4)
        self.device = device

    def copy(self, source, target, number, half_partner):
        send, recv = self.sems
        return pltpu.make_async_remote_copy(
            src_ref=source,
            dst_ref=target,
            send_sem=send.at[self.base + number],
            recv_sem=recv.at[self.base + number],
            device_id=self.device(half_partner),
            device_id_type=MESH,
        )

    def round_one(self):
        copies = []
        for half in range(2):
            partner = self.other[half]
            for slot, block in enumerate((partner, self.far)):
                copies.append(
                    self.copy(
                        self.blocks.at[block, half],
                        self.first.at[half, slot],
                        half * 2 + slot,
                        partner,
                    )
                )
        return copies

    def round_two(self):
        return [
            self.copy(self.outgoing.at[half], self.second.at[half], 4 + half, self.other[1 - half])
            for half in range(2)
        ]

    def start_one(self):
        for copy in self.round_one():
            copy.start()

    def start_two(self):
        for copy in self.round_one():
            copy.wait()
        for half in range(2):
            block = self.other[1 - half]
            self.outgoing[half] = (
                self.blocks[block, half].astype(jnp.float32)
                + self.first[half, 1].astype(jnp.float32)
            ).astype(jnp.bfloat16)
        for copy in self.round_two():
            copy.start()

    def finish(self):
        for copy in self.round_two():
            copy.wait()
        return [
            (
                self.blocks[self.index, half].astype(jnp.float32)
                + self.first[half, 0].astype(jnp.float32)
                + self.second[half].astype(jnp.float32)
            ).astype(jnp.bfloat16)
            for half in range(2)
        ]


class Gather:
    def __init__(self, send, recv, event, pack, tensor):
        self.send, self.recv = send, recv
        self.event, self.pack, self.tensor = event, pack, tensor
        self.core = lax.rem(event, 2)
        self.used = 0
        self.started = []
        self.partner = (event + 1 - 2 * self.core, pack, tensor)
        self.pair_started = []

    def copy(self, source, target, device):
        number = self.used
        self.used += 1
        copy = pltpu.make_async_remote_copy(
            src_ref=source,
            dst_ref=target,
            send_sem=self.send.at[number],
            recv_sem=self.recv.at[number],
            device_id=device,
            device_id_type=MESH,
        )
        copy.start()
        self.started.append(copy)
        return copy

    def along_tensor(self, shift):
        return (self.event, self.pack, lax.rem(self.tensor + shift + 4, 4))

    def along_x(self, shift):
        return (lax.rem(self.event + 2 * shift + 8, 8), self.pack, self.tensor)

    def along_z(self, shift):
        return (self.event, lax.rem(self.pack + shift + 8, 8), self.tensor)

    def to_pair(self, region, name):
        self.pair_started.append((name, self.copy(region, region, self.partner)))

    def await_pair(self, names):
        for name, copy in self.pair_started:
            if name in names:
                copy.wait_recv()

    def end(self):
        for copy in self.started:
            copy.wait_send()


class TensorRing:
    def __init__(self, gather, name, own, region, halves):
        self.gather, self.name, self.own = gather, name, own
        self.region, self.halves = region, halves

    def start(self):
        device = self.gather.along_tensor
        self.near = [
            self.gather.copy(self.own, self.region(2), device(1)),
            self.gather.copy(self.own, self.region(1), device(-1)),
        ]

    def relay(self):
        for copy in self.near:
            copy.wait_recv()
        device = self.gather.along_tensor
        plus, minus = self.halves
        self.far = []
        if plus is not False:
            self.far.append(self.gather.copy(self.region(2, plus), self.region(3, plus), device(1)))
        if minus is not False:
            self.far.append(
                self.gather.copy(self.region(1, minus), self.region(3, minus), device(-1))
            )
        self.gather.to_pair(self.region(pl.ds(1, 2)), self.name)

    def end(self):
        for copy in self.far:
            copy.wait_recv()
        self.gather.to_pair(self.region(pl.ds(3, 1)), self.name)


class SideRing:
    def __init__(self, gather, name, size, index, device, region, halves):
        self.gather, self.name, self.size, self.index = gather, name, size, index
        self.device, self.region, self.halves = device, region, halves
        self.step = 0
        self.flying = None

    def block(self, shift, half=None):
        return self.region(lax.rem(self.index + shift + self.size, self.size), half)

    def start(self):
        block = self.block(0)
        self.flying = [
            self.gather.copy(block, block, self.device(1)),
            self.gather.copy(block, block, self.device(-1)),
        ]
        self.step = 1

    def advance(self):
        for copy in self.flying:
            copy.wait_recv()
        step = self.step
        last = step == self.size // 2
        forward = []
        if not last:
            halves = (None, None) if step + 1 < self.size // 2 else self.halves
            for sign, half in zip((1, -1), halves):
                if half is not False:
                    block = self.block(-sign * step, half)
                    forward.append(self.gather.copy(block, block, self.device(sign)))
            for sign in (1, -1):
                self.gather.to_pair(self.block(-sign * step), self.name)
        else:
            self.gather.to_pair(self.block(step), self.name)
        self.flying = forward
        self.step = step + 1


def masks(documents, tensor):
    own = documents[:, pl.ds(pl.multiple_of(tensor * 128, 128), 128)].astype(jnp.float32)
    before = documents[
        :, pl.ds(pl.multiple_of(lax.rem(tensor + 3, 4) * 128, 128), 128)
    ].astype(jnp.float32)
    before = before - jnp.where(tensor == 0, 1000.0, 0.0)
    mine = jnp.broadcast_to(own, (128, 128)).T
    row = lax.broadcasted_iota(jnp.int32, (128, 128), 0)
    column = lax.broadcasted_iota(jnp.int32, (128, 128), 1)
    allowed = jnp.concatenate(
        [
            jnp.where(mine == before, 1.0, 0.0),
            jnp.where((mine == own) & (column <= row), 1.0, 0.0),
        ],
        axis=1,
    )
    root = jnp.sqrt(jnp.sum(allowed, axis=1, keepdims=True))
    return (allowed, root)


def by_parity(value):
    first = lax.rem(lax.broadcasted_iota(jnp.int32, value.shape, 1), 128) < 64
    return (
        jnp.where(first, value, 0.0).astype(jnp.bfloat16),
        jnp.where(first, 0.0, value).astype(jnp.bfloat16),
    )


def rounded(value):
    return value.astype(jnp.bfloat16).astype(jnp.float32)


def step_kernel(
    features,
    owner,
    slot,
    documents,
    out_grad,
    enc_hbm,
    first_hbm,
    second_hbm,
    attn_out_hbm,
    gate_hbm,
    up_hbm,
    down_z_hbm,
    down_t_hbm,
    packed_hbm,
    row_hbm,
    enc_grad,
    packed_out,
    row_grad,
    enc,
    first,
    second,
    attn_out,
    gate_in,
    up_in,
    down_z,
    down_t,
    preact,
    wide,
    send_rows,
    got_rows,
    send_slots,
    got_slots,
    back_rows,
    acts,
    cots,
    grads,
    firsts,
    seconds,
    outs,
    grads2,
    firsts2,
    seconds2,
    outs2,
    send_z,
    got_z,
    normed,
    query,
    keys,
    values,
    gates,
    attended,
    weights,
    slopes,
    slopes16,
    total_a,
    total_b,
    residual,
    normed2,
    allowed_ref,
    root_ref,
    d_proj,
    gated,
    halo_send,
    halo_got,
    load_sem,
    send_sem,
    recv_sem,
    ready_sem,
    gather_send,
    gather_recv,
    pair_send,
    pair_recv,
    half_send,
    half_recv,
    z_send,
    z_recv,
    halo_sem,
):
    event, pack, tensor = where_am_i()
    core = lax.rem(event, 2)
    chip_x = event // 2
    partner = (event + 1 - 2 * core, pack, tensor)
    bf16, f32 = jnp.bfloat16, jnp.float32
    barrier = pltpu.get_barrier_semaphore()
    loads = []
    for number, (source, target) in enumerate(
        (
            (enc_hbm.at[0], enc.at[0]),
            (enc_hbm.at[1], enc.at[1]),
            (first_hbm.at[pl.ds(0, 2)], first.at[0]),
            (second_hbm.at[pl.ds(2, 2)], second.at[0]),
            (attn_out_hbm, attn_out.at[0]),
            (gate_hbm.at[0], gate_in.at[0]),
            (up_hbm.at[1], up_in.at[0]),
            (down_z_hbm.at[0], down_z.at[0]),
            (down_t_hbm.at[1], down_t.at[0]),
        )
    ):
        load = pltpu.make_async_copy(source, target, load_sem.at[number])
        load.start()
        loads.append(load)
    for step in range(1, 8):
        for device in (
            (event, lax.rem(pack + step, 8), tensor),
            (lax.rem(event + step, 8), pack, tensor),
        ):
            pl.semaphore_signal(barrier, inc=1, device_id=device, device_id_type=MESH)
    for step in (1, 3):
        pl.semaphore_signal(
            barrier,
            inc=1,
            device_id=(event, pack, lax.rem(tensor + step, 4)),
            device_id_type=MESH,
        )
    picks = routing(owner[...].astype(f32))
    slot_row = slot[...].astype(f32) + 1.0
    lane = lax.broadcasted_iota(jnp.int32, (GROUPS, 128), 1)
    slots = jnp.full((GROUPS, 128), -1.0, f32)
    for k in range(CAP):
        value = jnp.sum(jnp.where(picks[k], slot_row, 0.0), axis=1, keepdims=True) - 1.0
        slots = jnp.where(lane == k, value, slots)
    send_slots[:, 0, :] = slots
    for k in range(CAP):
        spread_rows(wide, k, dot32(one_hot(picks[k]), features[...]))
    send_rows[...] = wide[...].astype(bf16).reshape(GROUPS, BLOCK_ROWS, 128)
    pl.semaphore_wait(barrier, 16)
    for step in range(1, 8):
        pl.semaphore_signal(
            ready_sem,
            inc=1,
            device_id=(lax.rem(event + step, 8), pack, tensor),
            device_id_type=MESH,
        )

    gather = Gather(gather_send, gather_recv, event, pack, tensor)
    whole = slice(None)
    low, high = pl.ds(0, 1), pl.ds(1, 1)
    foreign = pl.ds(1, 3)

    def part_of(half):
        return whole if half is None else half

    def first_at(where, index, half=None):
        return first.at[where, part_of(half), index, core]

    def second_at(where, index, half=None):
        return second.at[where, part_of(half), index, core]

    def attn_out_at(where, index, half=None):
        return attn_out.at[where, index, core, part_of(half)]

    def gate_at(where, index, half=None):
        return gate_in.at[where, index, core, part_of(half)]

    def down_z_at(where, index, half=None):
        return down_z.at[where, index, core]

    def up_at(where, half=None):
        return up_in.at[where, core, part_of(half)]

    def down_t_at(where, half=None):
        return down_t.at[where, core, part_of(half)]

    def slice_ring(name, own, region, index, halves):
        return TensorRing(
            gather, name, own, lambda where, half=None: region(where, index, half), halves
        )

    t_first = slice_ring(
        "attn", first_hbm.at[pl.ds(0, 2), chip_x, core], first_at, chip_x, (low, high)
    )
    t_second = slice_ring(
        "attn", second_hbm.at[pl.ds(2, 2), pack, core], second_at, pack, (low, high)
    )
    t_out = slice_ring("out", attn_out_hbm.at[chip_x, core], attn_out_at, chip_x, (low, high))
    t_gate = slice_ring("ffn", gate_hbm.at[0, chip_x, core], gate_at, chip_x, (low, high))
    t_down = slice_ring("ffn", down_z_hbm.at[0, pack, core], down_z_at, pack, (False, None))
    t_up = TensorRing(gather, "ffn", up_hbm.at[1, core], up_at, (low, high))
    t_last = TensorRing(gather, "ffn", down_t_hbm.at[1, core], down_t_at, (low, high))

    def side_ring(name, axis, region, halves):
        size, index, device = (
            (4, chip_x, gather.along_x) if axis == "x" else (8, pack, gather.along_z)
        )
        return SideRing(
            gather,
            name,
            size,
            index,
            device,
            lambda number, half=None: region(foreign, number, half),
            halves,
        )

    x_first = side_ring("attn", "x", first_at, (low, high))
    z_second = side_ring("attn", "z", second_at, (low, high))
    x_out = side_ring("out", "x", attn_out_at, (low, high))
    x_gate = side_ring("ffn", "x", gate_at, (low, high))
    z_down = side_ring("ffn", "z", down_z_at, (None, False))

    t_second.start()
    t_first.start()
    pl.semaphore_wait(ready_sem, 7)
    start_exchange(send_slots, got_slots, event, pack, tensor, send_sem.at[0], recv_sem.at[0])
    start_exchange(send_rows, got_rows, event, pack, tensor, send_sem.at[1], recv_sem.at[1])
    t_second.relay()
    t_first.relay()
    t_gate.start()
    t_out.start()
    t_down.start()
    t_second.end()
    z_second.start()
    t_first.end()
    x_first.start()
    t_gate.relay()
    t_out.relay()
    t_down.relay()
    t_up.start()
    allowed, root = masks(documents, tensor)
    allowed_ref[...] = allowed
    root_ref[...] = jnp.broadcast_to(root, (128, 128))

    def pair_copy(number, array):
        return pltpu.make_async_remote_copy(
            src_ref=array.at[0],
            dst_ref=array.at[1],
            send_sem=pair_send.at[number],
            recv_sem=pair_recv.at[number],
            device_id=partner,
            device_id_type=MESH,
        )

    end_exchange(send_slots, got_slots, send_sem.at[0], recv_sem.at[0])
    end_exchange(send_rows, got_rows, send_sem.at[1], recv_sem.at[1])
    wide[...] = got_rows[...].reshape(GROUPS * BLOCK_ROWS, 128).astype(f32)
    turned = jnp.concatenate([got_slots[:, 0, :], jnp.full((GROUPS, 128), -1.0, f32)], axis=0).T
    place = lax.broadcasted_iota(jnp.int32, (128, GROUPS), 0).astype(f32)
    total = None
    for k in range(CAP):
        pick = one_hot(turned[k : k + 1, :GROUPS] == place)
        term = dot32(pick, joined_rows(wide, k))
        total = term if total is None else total + term
    rows = total.astype(bf16)
    for load in loads[:2]:
        load.wait()
    pre = dot32(rows, enc[0])
    preact[...] = pre
    act = silu(pre).astype(bf16)
    quarter = rounded(dot32(act, enc[1]))
    normed_f, factor1 = norm_rows(quarter)
    halo_send[0] = normed_f.astype(bf16)
    normed[1] = normed_f.astype(bf16)
    residual[...] = quarter

    def halo_copy(number, target, shift):
        return pltpu.make_async_remote_copy(
            src_ref=halo_send.at[number],
            dst_ref=target,
            send_sem=halo_sem.at[number],
            recv_sem=halo_sem.at[2 + number],
            device_id=(event, pack, lax.rem(tensor + shift, 4)),
            device_id_type=MESH,
        )

    halo = halo_copy(0, normed.at[0], 1)
    halo.start()
    acts[0, 0] = rows
    acts[1, 0] = act
    act_copies = [pair_copy(layer, acts.at[layer]) for layer in range(2)]
    for copy in act_copies:
        copy.start()
    t_last.start()
    t_out.end()
    x_out.start()
    z_second.advance()
    t_gate.end()
    t_down.end()
    z_down.start()
    x_first.advance()
    x_gate.start()
    z_second.advance()
    x_out.advance()
    z_down.advance()
    x_first.advance()
    z_second.advance()
    z_down.advance()
    for load in loads[2:4]:
        load.wait()
    halo.wait()
    own_rows = normed[1]
    all_rows = normed[...].reshape(256, 1024)
    total_a[...] = quarter

    def matrix(slot_index, number):
        source = first if number < 2 else second
        return source[slot_index, number % 2].reshape(1024, 256)

    def attend(slot_index):
        query_f = rounded(dot32(own_rows, matrix(slot_index, 0)))
        gate = rounded(dot32(own_rows, matrix(slot_index, 3)))
        keys_f = rounded(dot32(all_rows, matrix(slot_index, 1)))
        values_f = rounded(dot32(all_rows, matrix(slot_index, 2)))
        gates[slot_index] = gate
        sides = []
        for ref, value in ((query, query_f), (keys, keys_f), (values, values_f)):
            pieces = by_parity(value)
            for parity in range(2):
                ref[slot_index, parity] = pieces[parity]
            sides.append(pieces)
        parts = []
        allowed = allowed_ref[...] > 0.5
        for pair in range(2):
            columns = slice(pair * 128, (pair + 1) * 128)
            part = None
            for parity in range(2):
                scores = (
                    dot32(sides[0][parity][:, columns], sides[1][parity][:, columns], ((1,), (1,)))
                    * HEAD_SCALE
                )
                sigma = jax.nn.sigmoid(scores)
                weight = jnp.where(allowed, scores * sigma, 0.0).astype(bf16)
                weights[slot_index, pair * 2 + parity] = weight
                slopes[slot_index, pair * 2 + parity] = jnp.where(
                    allowed, sigma * (1.0 + scores * (1.0 - sigma)), 0.0
                )
                term = dot32(weight, sides[2][parity][:, columns])
                part = term if part is None else part + term
            parts.append(part)
        result = jnp.concatenate(parts, axis=1) / root_ref[:, 0:1]
        attended[slot_index] = result
        gated[slot_index] = (result * silu(gate)).astype(bf16)

    attend(0)
    t_up.relay()
    z_second.advance()
    gather.await_pair(("attn",))
    x_gate.advance()
    z_down.advance()
    attend(1)
    x_out.advance()
    attend(2)
    t_last.relay()
    z_down.advance()
    attend(3)
    gather.await_pair(("out",))
    loads[4].wait()
    for slot_index in range(4):
        total_a[...] += rounded(
            dot32(gated[slot_index], attn_out[slot_index].reshape(256, 1024))
        )
    resid = rounded(total_a[...])
    normed2_f, factor2 = norm_rows(resid)
    normed2[...] = normed2_f.astype(bf16)
    total_a[...] = resid
    total_b[...] = jnp.zeros((128, 1024), f32)

    def feed(slot_index, carry):
        rows = normed2[...]
        gate = dot32(rows, gate_in[slot_index].reshape(1024, 512))
        upper = dot32(rows, up_in[slot_index].reshape(1024, 512))
        sigma = jax.nn.sigmoid(gate)
        active = gate * sigma
        down = (down_z[slot_index].reshape(256, 1024), down_t[slot_index].reshape(256, 1024))
        hidden = (active * upper).astype(bf16)
        total_a[...] += rounded(dot32(hidden[:, :256], down[0]) + dot32(hidden[:, 256:], down[1]))
        d_hidden = jnp.concatenate(
            [dot32(out_grad[...], part, ((1,), (1,))) for part in down], axis=1
        )
        d_gate = (d_hidden * upper * (sigma * (1.0 + gate * (1.0 - sigma)))).astype(bf16)
        d_upper = (d_hidden * active).astype(bf16)
        total_b[...] += rounded(
            dot32(d_gate, gate_in[slot_index].reshape(1024, 512), ((1,), (1,)))
            + dot32(d_upper, up_in[slot_index].reshape(1024, 512), ((1,), (1,)))
        )
        return carry

    for load in loads[5:]:
        load.wait()
    feed(0, 0)
    x_gate.advance()
    t_up.end()
    t_last.end()
    gather.await_pair(("ffn",))
    lax.fori_loop(1, 4, feed, 0)
    packed_out[...] = total_a[...].astype(bf16)
    stores = [
        pltpu.make_async_copy(packed_out, packed_hbm, load_sem.at[0]),
        pltpu.make_async_copy(row_grad, row_hbm, load_sem.at[1]),
    ]
    stores[0].start()
    d_resid = (
        out_grad[...].astype(f32) + norm_back(total_b[...], normed2_f, factor2)
    ).astype(bf16)
    total_a[...] = jnp.zeros((128, 1024), f32)
    total_b[...] = jnp.zeros((128, 1024), f32)

    def attend_back(slot_index, carry):
        gate = gates[slot_index]
        d_gated = dot32(d_resid, attn_out[slot_index].reshape(256, 1024), ((1,), (1,)))
        sigma = jax.nn.sigmoid(gate)
        d_attended = by_parity(d_gated * (gate * sigma) / root_ref[:, 0:1])
        d_gate = (
            d_gated * attended[slot_index] * (sigma * (1.0 + gate * (1.0 - sigma)))
        ).astype(bf16)
        d_parts = [[], []]
        for pair in range(2):
            columns = slice(pair * 128, (pair + 1) * 128)
            sums = [None, None]
            for parity in range(2):
                head = pair * 2 + parity
                d_side = d_attended[parity][:, columns]
                d_weights = dot32(d_side, values[slot_index, parity, :, columns], ((1,), (1,)))
                d_scores = (d_weights * slopes[slot_index, head]).astype(bf16)
                slopes16[slot_index, head] = d_scores
                terms = (
                    dot32(d_scores, query[slot_index, parity, :, columns], ((0,), (0,))),
                    dot32(weights[slot_index, head], d_side, ((0,), (0,))),
                )
                for number, term in enumerate(terms):
                    sums[number] = term if sums[number] is None else sums[number] + term
            d_parts[0].append(sums[0] * HEAD_SCALE)
            d_parts[1].append(sums[1])
        d_keys, d_values = (
            jnp.concatenate(parts, axis=1).astype(bf16) for parts in d_parts
        )
        for number, value in enumerate((d_keys[128:], d_values[128:], d_gate)):
            d_proj[slot_index, number] = value
        total_b[...] += dot32(d_keys[:128], matrix(slot_index, 1), ((1,), (1,))) + dot32(
            d_values[:128], matrix(slot_index, 2), ((1,), (1,))
        )
        return carry

    lax.fori_loop(0, 4, attend_back, 0)
    halo_send[1] = total_b[...].astype(bf16)
    halo_back = halo_copy(1, halo_got, 3)
    halo_back.start()

    def project_back(slot_index, carry):
        parts = []
        for pair in range(2):
            columns = slice(pair * 128, (pair + 1) * 128)
            parts.append(
                (
                    dot32(slopes16[slot_index, pair * 2], keys[slot_index, 0, :, columns])
                    + dot32(slopes16[slot_index, pair * 2 + 1], keys[slot_index, 1, :, columns])
                )
                * HEAD_SCALE
            )
        d_query = jnp.concatenate(parts, axis=1).astype(bf16)
        total_a[...] += dot32(d_query, matrix(slot_index, 0), ((1,), (1,))) + sum(
            dot32(d_proj[slot_index, number - 1], matrix(slot_index, number), ((1,), (1,)))
            for number in range(1, 4)
        )
        return carry

    lax.fori_loop(0, 4, project_back, 0)
    halo_back.wait()
    d_normed = total_a[...] + halo_got[...].astype(f32)
    normed_f, factor1 = norm_rows(residual[...])
    d_quarter = (d_resid.astype(f32) + norm_back(d_normed, normed_f, factor1)).astype(bf16)
    cots[1, 0] = d_quarter
    cot_copies = [pair_copy(2 + layer, cots.at[layer]) for layer in range(2)]
    cot_copies[1].start()
    cots[0, 0] = (
        dot32(d_quarter, enc[1], ((1,), (1,))) * silu_grad(preact[...])
    ).astype(bf16)
    cot_copies[0].start()
    for copy in act_copies:
        copy.wait()

    def tensor_device(index):
        return (event, pack, index)

    def chip_device(index):
        return (index * 2 + core, pack, tensor)

    rings = ((tensor, tensor_device), (chip_x, chip_device))
    stages = [[], []]
    for unit in range(4):
        for stage, refs in enumerate(
            ((grads, firsts, seconds, outs), (grads2, firsts2, seconds2, outs2))
        ):
            index, device = rings[stage if unit < 3 else 1 - stage]
            stages[stage].append(
                Halving(
                    *(ref.at[unit] for ref in refs),
                    (half_send, half_recv),
                    (stage * 4 + unit) * 6,
                    index,
                    device,
                )
            )
    for layer in (1, 0):
        cot_copies[layer].wait()
        cot = cots[layer].reshape(256, 1024)
        units = (0, 1) if layer == 1 else (2, 3)
        for chip in range(4):
            columns = pl.ds(pl.multiple_of((chip * 2 + core) * 128, 128), 128)
            act = acts[layer, :, :, columns].reshape(256, 128)
            term = dot32(act, cot, ((0,), (0,))).astype(bf16)
            for block in range(4):
                for half in range(2):
                    for part in range(2):
                        low_row = half * 64 + part * 32
                        piece = term[low_row : low_row + 32, block * 256 : (block + 1) * 256]
                        if units[part] < 3:
                            grads[units[part], block, half, chip] = piece
                        else:
                            grads[units[part], chip, half, block] = piece
        for unit in units:
            stages[0][unit].start_one()
    lane = lax.broadcasted_iota(jnp.int32, (GROUPS, 128), 1).astype(jnp.float32)
    for k in range(CAP):
        chosen = one_hot(got_slots[:, 0, k : k + 1] == lane)
        spread_rows(wide, k, dot32(chosen, d_quarter))
    send_rows[...] = wide[...].astype(bf16).reshape(GROUPS, BLOCK_ROWS, 128)
    start_exchange(send_rows, back_rows, event, pack, tensor, send_sem.at[2], recv_sem.at[2])
    for unit in range(4):
        stages[0][unit].start_two()
    for unit in range(4):
        for half, value in enumerate(stages[0][unit].finish()):
            for block in range(4):
                grads2[unit, block, half] = value[block]
        stages[1][unit].start_one()
    for unit in range(4):
        stages[1][unit].start_two()
    for unit in range(4):
        for half, value in enumerate(stages[1][unit].finish()):
            for number in range(2):
                send_z[half * 4 + unit % 2 * 2 + number, 1 - unit // 2] = value[
                    number * 16 : (number + 1) * 16
                ]
    z_copies = []
    for step in (1, 7, 2, 6, 3, 5, 4):
        other = lax.rem(pack + step, 8)
        z_copies.append(
            pltpu.make_async_remote_copy(
                src_ref=send_z.at[other],
                dst_ref=got_z.at[pack],
                send_sem=z_send.at[step],
                recv_sem=z_recv.at[step],
                device_id=(event, other, tensor),
                device_id_type=MESH,
            )
        )
        z_copies[-1].start()
    got_z[pack] = send_z[pack]
    end_exchange(send_rows, back_rows, send_sem.at[2], recv_sem.at[2])
    wide[...] = back_rows[...].reshape(GROUPS * BLOCK_ROWS, 128).astype(f32)
    total = None
    for k in range(CAP):
        term = dot32(one_hot(picks[k]), joined_rows(wide, k), ((0,), (0,)))
        total = term if total is None else total + term
    row_grad[...] = total.astype(bf16)
    stores[1].start()
    gather.end()
    for copy in z_copies:
        copy.wait()
    total = got_z[0].astype(jnp.float32)
    for source in range(1, 8):
        total = total + got_z[source].astype(jnp.float32)
    enc_grad[...] = total
    for store in stores:
        store.wait()


def hand_over(packed_in, row_in, enc_in, packed_out, row_out, enc_out):
    packed_out[...] = packed_in[...]
    row_out[...] = row_in[...]
    enc_out[...] = enc_in[...]


def shards(
    features,
    dest_owner,
    dest_slot,
    doc_ids,
    enc_weight,
    attn_in,
    attn_out,
    ffn_in,
    ffn_out,
    out_grad,
):
    bf16, f32 = jnp.bfloat16, jnp.float32
    vmem = pl.BlockSpec(memory_space=pltpu.VMEM)
    hbm = pl.BlockSpec(memory_space=pl.ANY)
    dma = pltpu.SemaphoreType.DMA
    packed_out, row_grad, enc_grad = pl.pallas_call(
        step_kernel,
        out_shape=(
            jax.ShapeDtypeStruct((128, 1024), bf16),
            jax.ShapeDtypeStruct((128, 1024), bf16),
            jax.ShapeDtypeStruct((2, 16, 256), f32),
        ),
        in_specs=[vmem] * 5 + [hbm] * 8,
        out_specs=(hbm, hbm, vmem),
        scratch_shapes=[
            pltpu.VMEM((128, 1024), bf16),
            pltpu.VMEM((128, 1024), bf16),
            pltpu.VMEM((2, 1024, 1024), bf16),
            pltpu.VMEM((4, 2, 4, 2, 128, 256), bf16),
            pltpu.VMEM((4, 2, 8, 2, 64, 256), bf16),
            pltpu.VMEM((4, 4, 2, 2, 16, 1024), bf16),
            pltpu.VMEM((4, 4, 2, 2, 64, 512), bf16),
            pltpu.VMEM((4, 2, 2, 256, 512), bf16),
            pltpu.VMEM((4, 8, 2, 16, 1024), bf16),
            pltpu.VMEM((4, 2, 2, 64, 1024), bf16),
            pltpu.VMEM((128, 1024), f32),
            pltpu.VMEM((GROUPS * BLOCK_ROWS, 128), f32),
            pltpu.VMEM((GROUPS, BLOCK_ROWS, 128), bf16),
            pltpu.VMEM((GROUPS, BLOCK_ROWS, 128), bf16),
            pltpu.VMEM((GROUPS, 1, 128), f32),
            pltpu.VMEM((GROUPS, 1, 128), f32),
            pltpu.VMEM((GROUPS, BLOCK_ROWS, 128), bf16),
            pltpu.VMEM((2, 2, 128, 1024), bf16),
            pltpu.VMEM((2, 2, 128, 1024), bf16),
            pltpu.VMEM((4, 4, 2, 4, 32, 256), bf16),
            pltpu.VMEM((4, 2, 2, 4, 32, 256), bf16),
            pltpu.VMEM((4, 2, 4, 32, 256), bf16),
            pltpu.VMEM((4, 2, 4, 32, 256), bf16),
            pltpu.VMEM((4, 4, 2, 32, 256), bf16),
            pltpu.VMEM((4, 2, 2, 32, 256), bf16),
            pltpu.VMEM((4, 2, 32, 256), bf16),
            pltpu.VMEM((4, 2, 32, 256), bf16),
            pltpu.VMEM((8, 2, 16, 256), bf16),
            pltpu.VMEM((8, 2, 16, 256), bf16),
            pltpu.VMEM((2, 128, 1024), bf16),
            pltpu.VMEM((4, 2, 128, 256), bf16),
            pltpu.VMEM((4, 2, 256, 256), bf16),
            pltpu.VMEM((4, 2, 256, 256), bf16),
            pltpu.VMEM((4, 128, 256), f32),
            pltpu.VMEM((4, 128, 256), f32),
            pltpu.VMEM((4, 4, 128, 256), bf16),
            pltpu.VMEM((4, 4, 128, 256), f32),
            pltpu.VMEM((4, 4, 128, 256), bf16),
            pltpu.VMEM((128, 1024), f32),
            pltpu.VMEM((128, 1024), f32),
            pltpu.VMEM((128, 1024), f32),
            pltpu.VMEM((128, 1024), bf16),
            pltpu.VMEM((128, 256), f32),
            pltpu.VMEM((128, 128), f32),
            pltpu.VMEM((4, 3, 128, 256), bf16),
            pltpu.VMEM((4, 128, 256), bf16),
            pltpu.VMEM((2, 128, 1024), bf16),
            pltpu.VMEM((128, 1024), bf16),
            dma((9,)),
            dma((3,)),
            dma((3,)),
            pltpu.SemaphoreType.REGULAR,
            dma((96,)),
            dma((96,)),
            dma((4,)),
            dma((4,)),
            dma((48,)),
            dma((48,)),
            dma((8,)),
            dma((8,)),
            dma((4,)),
        ],
        compiler_params=pltpu.CompilerParams(
            collective_id=0, has_side_effects=True, vmem_limit_bytes=VMEM_LIMIT
        ),
        name="train_step",
    )(
        features,
        dest_owner.reshape(1, 128),
        dest_slot.reshape(1, 128),
        doc_ids,
        out_grad[0],
        enc_weight,
        attn_in.reshape(4, 4, 2, 128, 256),
        attn_in.reshape(4, 8, 2, 64, 256),
        attn_out.reshape(4, 2, 2, 16, 1024),
        ffn_in.reshape(2, 4, 2, 2, 64, 512),
        ffn_in.reshape(2, 2, 2, 256, 512),
        ffn_out.reshape(2, 8, 2, 16, 1024),
        ffn_out.reshape(2, 2, 2, 64, 1024),
    )
    packed_out, row_grad, enc_grad = pl.pallas_call(
        hand_over,
        out_shape=(
            jax.ShapeDtypeStruct((128, 1024), bf16),
            jax.ShapeDtypeStruct((128, 1024), bf16),
            jax.ShapeDtypeStruct((2, 16, 256), f32),
        ),
        in_specs=[vmem] * 3,
        out_specs=(vmem, vmem, vmem),
        name="hand_over",
    )(packed_out, row_grad, enc_grad)
    return (packed_out[None], row_grad, enc_grad)


def solution(mesh):
    placed = (
        P(("event", "pack", "tensor"), None),
        P(("event", "pack", "tensor")),
        P(("event", "pack", "tensor")),
        P(("event", "pack"), None),
        P(),
        P(None, None, "tensor"),
        P("tensor", None),
        P(None, None, "tensor"),
        P("tensor", None),
        P(("event", "pack"), "tensor", None),
    )
    return jax.shard_map(
        shards,
        mesh=mesh,
        in_specs=placed,
        out_specs=(
            P(("event", "pack"), "tensor", None),
            P(("event", "pack", "tensor"), None),
            P(None, ("event", "pack"), "tensor"),
        ),
        check_vma=False,
    )
```
